128 devices in a mesh: slab: 16 (over z_lo, x, core), buddy: 8 (over y, z_hi).
Axes of the slice: x: 4, y: 4, z: 4 (z_hi: 2, z_lo: 2; z = z_hi * 2 + z_lo), core: 2. Of those that a mesh axis runs over, the one named last changes fastest.
Arguments:
- checkpoint: float32 [64, 5, 128, 4, 256], P('buddy', None, 'slab'), may hold values from -6 to 6
- slot_block: int32 [8, 8], replicated, may hold values from 0 to 63, as said below
- live_state: float32 [8, 5, 128, 32, 256], P('buddy', None, 'slab'), may hold values from -6 to 6
- levels: int32 [2, 8, 3], P(None, 'buddy'), may hold values from 0 to 2
- coefficients: float32 [2, 8], P(None, 'buddy'), may hold values from 0.3 to 1
- tile_owner: int32 [16, 16], P('slab'), may hold values from 0 to 7, as said below
Outputs:
- recovered: float32 [8, 5, 128, 32, 256], P('buddy', None, 'slab')
- combined: float32 [32, 5, 128, 2, 256], P('buddy', None, 'slab')
The draws below stay inside these ranges and needn't reach their ends.
Inputs may be any that keep to these rules, and one draw needn't show every extreme that they name: `slot_block`: row h lists the blocks in the 8 slots of holder h, block j of grid g written g * 8 + j. Every block is held exactly once, never by its own grid's holder; one holder keeps at most 3 blocks of one grid, and some holder keeps exactly 3 of some grid. `tile_owner`: no reader reads more than 4 tiles of one slab, and in every slab some reader reads exactly 4.
All inputs are finite; a program needn't handle non-finite values.
Results may differ from the reference program's by a relative error of at most 0.000096.
Values sent between devices are 32-bit elements; how exact they have to be, the bound alone decides.
A program may use at most 192 MiB of HBM per device.

```python
import jax
import jax.numpy as jnp

CX = 256
CY = 32
CZ = 8
BLOCKS = 8
HELD_MOST = 3
TILE_LINES = 2
GRIDS = 8
SLABS = 16
NZ = 128
BLOCK_LINES = 4
TILES = 16
READ_MOST = 4


def draw_slot_block(key, part):
    key_place, key_offset, key_slots, key_blocks = jax.random.split(key, 4)
    placing = jax.random.permutation(key_place, GRIDS).astype(jnp.int32)
    position = jnp.zeros((GRIDS,), jnp.int32).at[placing].set(jnp.arange(GRIDS, dtype=jnp.int32))
    offset = jax.random.randint(key_offset, (), 0, GRIDS - 1).astype(jnp.int32)
    shift_group = jax.vmap(lambda sub_key: jax.random.permutation(sub_key, BLOCKS))(jax.random.split(key_slots, GRIDS)).astype(jnp.int32)
    block_order = jax.vmap(lambda sub_key: jax.random.permutation(sub_key, BLOCKS))(jax.random.split(key_blocks, GRIDS)).astype(jnp.int32)
    shifts = 1 + (shift_group // HELD_MOST + offset) % (GRIDS - 1)
    owners = placing[(position[:, None] - shifts) % GRIDS]
    chosen_blocks = block_order[owners, shift_group]
    return (owners * BLOCKS + chosen_blocks).astype(jnp.int32)


def draw_tile_owner(key, part):

    def one_slab(slab_key):
        key_tiles, key_readers = jax.random.split(slab_key)
        tile_order = jax.random.permutation(key_tiles, TILES).astype(jnp.int32)
        readers = jax.random.permutation(key_readers, GRIDS).astype(jnp.int32)
        counter = jnp.arange(TILES, dtype=jnp.int32)
        others = (counter - READ_MOST) % (GRIDS - 1) + 1
        chosen = jnp.where(counter < READ_MOST, readers[0], readers[others])
        return jnp.zeros((TILES,), jnp.int32).at[tile_order].set(chosen.astype(jnp.int32))
    return jax.vmap(one_slab)(jax.random.split(key, SLABS))


def plant(drawn, own_key, least, largest):
    extent = drawn.shape
    spot = [jax.random.randint(jax.random.fold_in(own_key, axis), (), 0, extent[axis]) for axis in range(len(extent))]
    drawn = drawn.at[tuple(spot)].set(least)
    longest = extent.index(max(extent))
    spot[longest] = (spot[longest] + 1) % extent[longest]
    return drawn.at[tuple(spot)].set(largest)


def block_levels(stream_key, dims, cuts, low, top_value):
    factor_of, own = 1.0, jax.random.fold_in(stream_key, 6)
    for axis_at, parts in cuts:
        steps = jnp.exp(jax.random.uniform(jax.random.fold_in(own, axis_at), (parts,), jnp.float32, low / len(cuts), top_value / len(cuts)))
        factor_of = factor_of * jnp.repeat(steps, dims[axis_at] // parts).reshape([-1 if axis == axis_at else 1 for axis in range(len(dims))])
    return factor_of


def gaussian(stream_key, shape, deviation, limit, cuts=(), kind=jnp.bfloat16):
    entries = jax.random.normal(stream_key, shape, jnp.float32) * deviation
    if len(cuts) > 0:
        entries = block_levels(stream_key, shape, cuts, -0.22, 0.18) * entries
    return jnp.clip(entries, min=-limit, max=limit).astype(kind)


def setup_inputs(seed: int = 0) -> dict:
    key_of = jax.random.split(jax.random.key(seed), 7)
    checkpoint = gaussian(key_of[0], (GRIDS * BLOCKS, 5, NZ, BLOCK_LINES, CX), 1.0, 6.0, ((0, 8), (2, 16)), jnp.float32)
    slot_block = draw_slot_block(jax.random.fold_in(key_of[6], 71), 0)
    live_state = gaussian(key_of[2], (GRIDS, 5, NZ, CY, CX), 1.0, 6.0, ((0, 8), (2, 16)), jnp.float32)
    levels = plant(jax.random.randint(key_of[3], (2, GRIDS, 3), 0, 3), jax.random.fold_in(key_of[3], 1), 0, 2).astype(jnp.int32)
    coefficients = jnp.clip(0.3 + 0.7 * jax.random.uniform(key_of[4], (2, GRIDS), jnp.float32) ** block_levels(key_of[4], (2, GRIDS), ((1, 8),), -0.2, 0.2), 0.3, 1.0)
    tile_owner = draw_tile_owner(jax.random.fold_in(key_of[6], 71), 0)
    return {"checkpoint": checkpoint, "slot_block": slot_block, "live_state": live_state, "levels": levels, "coefficients": coefficients, "tile_owner": tile_owner}


VELOCITY = (0.3, -0.2, 0.45)
COURANT = 1.0


def apply_matrix(difference, axis_number):
    drift_speed = VELOCITY[axis_number]
    channels = [difference[..., channel_index, :, :, :] for channel_index in range(5)]
    pressure = channels[4]
    normal_velocity = channels[1 + axis_number]
    result = [drift_speed * channels[0] + normal_velocity, drift_speed * channels[1], drift_speed * channels[2], drift_speed * channels[3], drift_speed * pressure + normal_velocity]
    result[1 + axis_number] = result[1 + axis_number] + pressure
    return jnp.stack(result, axis=-4)


def direction_rate(plus_side, minus_side, middle, inv_spacing, axis_number):
    wave_speed = abs(VELOCITY[axis_number]) + 1.0
    flux_term = apply_matrix(plus_side - minus_side, axis_number)
    return inv_spacing * (0.5 * flux_term - (0.5 * wave_speed) * (plus_side + minus_side - 2.0 * middle))


def section_rate(padded, inv_spacing):
    middle = padded[..., 1:-1, :, :]
    summed_rate = direction_rate(jnp.roll(middle, -1, -1), jnp.roll(middle, 1, -1), middle, inv_spacing[0], 0)
    summed_rate = summed_rate + direction_rate(jnp.roll(middle, -1, -2), jnp.roll(middle, 1, -2), middle, inv_spacing[1], 1)
    summed_rate = summed_rate + direction_rate(padded[..., 2:, :, :], padded[..., :-2, :, :], middle, inv_spacing[2], 2)
    return -summed_rate


def spacing_terms(level_rows):
    inverse = jnp.exp2(level_rows.astype(jnp.float32))
    count_rows = level_rows.shape[0]
    members = tuple(inverse[:, axis_number].reshape(count_rows, 1, 1, 1, 1) for axis_number in range(3))
    denominator = (abs(VELOCITY[0]) + 1.0) * members[0] + (abs(VELOCITY[1]) + 1.0) * members[1]
    denominator = denominator + (abs(VELOCITY[2]) + 1.0) * members[2]
    return members, COURANT / denominator


def advance(state, inv_spacing, time_step, widen):
    first_rate = section_rate(widen(state), inv_spacing)
    second_rate = section_rate(widen(state + (0.5 * time_step) * first_rate), inv_spacing)
    third_rate = section_rate(widen(state + (0.5 * time_step) * second_rate), inv_spacing)
    fourth_rate = section_rate(widen(state + time_step * third_rate), inv_spacing)
    return state + (time_step / 6.0) * (first_rate + 2.0 * second_rate + 2.0 * third_rate + fourth_rate)


def wrap_layers(state):
    return jnp.concatenate([state[:, :, -1:], state, state[:, :, :1]], axis=2)


def reference(checkpoint, slot_block, live_state, levels, coefficients, tile_owner):
    flat_ids = slot_block.reshape(-1).astype(jnp.int32)
    ordered = jnp.zeros_like(checkpoint).at[flat_ids].set(checkpoint)
    restored = ordered.reshape(GRIDS, BLOCKS, 5, NZ, BLOCK_LINES, CX).transpose(0, 2, 3, 1, 4, 5).reshape(GRIDS, 5, NZ, CY, CX)
    lost_spacing, lost_step = spacing_terms(levels[0])
    live_spacing, live_step = spacing_terms(levels[1])
    recovered = advance(restored, lost_spacing, lost_step, wrap_layers)
    advanced = advance(live_state, live_spacing, live_step, wrap_layers)
    weighted = coefficients[0].reshape(GRIDS, 1, 1, 1, 1) * recovered + coefficients[1].reshape(GRIDS, 1, 1, 1, 1) * advanced
    summed = jnp.sum(weighted, axis=0)
    tiles = summed.reshape(5, SLABS, CZ, TILES, TILE_LINES, CX).transpose(1, 3, 0, 2, 4, 5)
    hits = (tile_owner[:, :, None] == jnp.arange(GRIDS, dtype=jnp.int32)[None, None, :]).astype(jnp.int32)
    before = jnp.cumsum(hits, axis=1) - hits
    ranks = jnp.sum(before * hits, axis=2).astype(jnp.int32)
    slab_index = jnp.broadcast_to(jnp.arange(SLABS, dtype=jnp.int32)[:, None], (SLABS, TILES))
    placed = jnp.zeros((GRIDS, READ_MOST, SLABS, 5, CZ, TILE_LINES, CX), summed.dtype)
    placed = placed.at[tile_owner.astype(jnp.int32), ranks, slab_index].set(tiles)
    combined = placed.transpose(0, 1, 3, 2, 4, 5, 6).reshape(GRIDS * READ_MOST, 5, SLABS * CZ, TILE_LINES, CX)
    return recovered, combined
```

```python
import functools

import jax
import jax.numpy as jnp
from jax import lax
from jax.experimental import pallas as pl
from jax.experimental.pallas import tpu as pltpu
from jax.sharding import PartitionSpec as P

MESH = pl.DeviceIdType.MESH
VELOCITY = (0.3, -0.2, 0.45)
FIELDS = 5
CZ = 8
CY = 32
CX = 256
HALO = 4
PEERS = 7
OFFSETS = ((2, 1), (2, 0), (1, 1), (3, 1), (0, 1), (1, 0), (3, 0))


def stencil(levels_ref, kind):
    inverse = []
    for axis in range(3):
        level = levels_ref[kind, 0, axis]
        inverse.append(jnp.where(level == 0, 1.0, jnp.where(level == 1, 2.0, 4.0)).astype(jnp.float32))
    denominator = (abs(VELOCITY[0]) + 1.0) * inverse[0] + (abs(VELOCITY[1]) + 1.0) * inverse[1]
    denominator = denominator + (abs(VELOCITY[2]) + 1.0) * inverse[2]
    step = jnp.max(1.0 / jnp.full((8, 128), denominator, jnp.float32))
    middle = -step * denominator
    sides = []
    for axis in range(3):
        scaled = step * inverse[axis]
        half = 0.5 * (abs(VELOCITY[axis]) + 1.0)
        sides.append(
            (
                scaled * (half - 0.5 * VELOCITY[axis]),
                scaled * (half + 0.5 * VELOCITY[axis]),
                scaled * -0.5,
            )
        )
    return middle, sides


def section(source, base, scalars, share, first, last, write):
    middle, sides = scalars
    middle = middle * share
    sides = [tuple(value * share for value in side) for side in sides]

    def one_layer(z, carry):
        def own_terms(field):
            q = source[field, z]
            out = base[field, z] + middle * q
            shifted = (
                (pltpu.roll(q, CX - 1, 1), pltpu.roll(q, 1, 1)),
                (pltpu.roll(q, CY - 1, 0), pltpu.roll(q, 1, 0)),
                (source[field, z + 1], source[field, z - 1]),
            )
            for (plus, minus), side in zip(shifted, sides):
                out = out + (side[0] * plus + side[1] * minus)
            return out, shifted

        pressure, around = own_terms(4)
        pushes = [side[2] * (plus - minus) for (plus, minus), side in zip(around, sides)]
        spread = None
        results = [None] * FIELDS
        for axis in range(3):
            out, around = own_terms(1 + axis)
            results[1 + axis] = out + pushes[axis]
            part = sides[axis][2] * (around[axis][0] - around[axis][1])
            spread = part if spread is None else spread + part
        results[4] = pressure + spread
        results[0] = own_terms(0)[0] + spread
        write(z, results)
        return carry

    lax.fori_loop(first, last, one_layer, 0)


def kernel(
    inverse_ref,
    tiles_ref,
    levels_ref,
    coefficients_ref,
    checkpoint_ref,
    live_ref,
    recovered_ref,
    combined_ref,
    lines_0,
    lines_1,
    lines_2,
    lines_3,
    lines_4,
    packed,
    lost,
    live,
    stage_a,
    stage_b,
    advanced,
    recovered,
    weighted,
    arrived,
    total,
    chosen,
    local_sem,
    send1,
    recv1,
    send2,
    recv2,
    send3,
    recv3,
    send4,
    recv4,
    halo_send,
    halo_recv,
    live_send,
    live_recv,
):
    lines = (lines_0, lines_1, lines_2, lines_3, lines_4)
    slab = lax.axis_index("slab")
    me = lax.axis_index("buddy")
    slabs = lax.axis_size("slab")
    row, half = me // 2, me % 2
    above = (slab + 1) % slabs
    below = (slab + slabs - 1) % slabs

    def at(offset):
        return ((row + offset[0]) % 4) * 2 + (half + offset[1]) % 2

    peers = [at(offset) for offset in OFFSETS]
    sources = [at(((4 - offset[0]) % 4, offset[1])) for offset in OFFSETS]

    live_in = pltpu.make_async_copy(live_ref.at[0], live.at[:, pl.ds(HALO, CZ)], local_sem.at[0])
    live_in.start()
    own_copies = []
    for field in range(FIELDS):
        copy = pltpu.make_async_copy(
            checkpoint_ref.at[:, field, me], lines[field].at[pl.ds(me * 8, 8)], local_sem.at[1 + field]
        )
        copy.start()
        own_copies.append(copy)

    barrier = pltpu.get_barrier_semaphore()
    for peer in peers:
        pl.semaphore_signal(barrier, inc=1, device_id={"buddy": peer}, device_id_type=MESH)
    for neighbour in (below, above):
        pl.semaphore_signal(barrier, inc=1, device_id={"slab": neighbour}, device_id_type=MESH)
    pl.semaphore_wait(barrier, PEERS + 2)

    first_copies = []
    for field in range(FIELDS):
        for i, peer in enumerate(peers):
            copy = pltpu.make_async_remote_copy(
                src_ref=checkpoint_ref.at[:, field, peer],
                dst_ref=lines[field].at[pl.ds(me * 8, 8)],
                send_sem=send1.at[field, i],
                recv_sem=recv1.at[field, i],
                device_id={"buddy": peer},
                device_id_type=MESH,
            )
            copy.start()
            first_copies.append(copy)
    live_copies = []
    for way, (neighbour, start, to) in enumerate(((below, 0, HALO + CZ), (above, CZ - HALO, 0))):
        copy = pltpu.make_async_remote_copy(
            src_ref=live_ref.at[0, :, pl.ds(start, HALO)],
            dst_ref=live.at[:, pl.ds(to, HALO)],
            send_sem=live_send.at[way],
            recv_sem=live_recv.at[way],
            device_id={"slab": neighbour},
            device_id_type=MESH,
        )
        copy.start()
        live_copies.append(copy)

    second_copies = []
    for field in range(FIELDS):
        own_copies[field].wait()
        for i in range(PEERS):
            first_copies[field * PEERS + i].wait_recv()
        for i, peer in enumerate(peers):
            for block in range(8):
                packed[field, i, pl.ds(block * 4, 4), :] = lines[field][inverse_ref[peer * 8 + block]]
            copy = pltpu.make_async_remote_copy(
                src_ref=packed.at[field, i],
                dst_ref=lost.at[field, HALO + me],
                send_sem=send2.at[field, i],
                recv_sem=recv2.at[field, i],
                device_id={"buddy": peer},
                device_id_type=MESH,
            )
            copy.start()
            second_copies.append(copy)
        for block in range(8):
            lost[field, HALO + me, pl.ds(block * 4, 4), :] = lines[field][inverse_ref[me * 8 + block]]

    def to_buffer(buffer):
        def write(z, results):
            for field in range(FIELDS):
                buffer[field, z] = results[field]

        return write

    def to_advanced(z, results):
        for field in range(FIELDS):
            advanced[z - HALO, field] = results[field]

    share = coefficients_ref[0, 0]
    live_share = coefficients_ref[1, 0]

    def to_recovered(z, results):
        for field in range(FIELDS):
            recovered[field, z - HALO] = results[field]
            weighted[z - HALO, field] = share * results[field] + live_share * advanced[z - HALO, field]

    def run_sections(state, scalars, finish, between):
        section(state, state, scalars, 0.25, 1, 2 * HALO + CZ - 1, to_buffer(stage_a))
        between(0)
        section(stage_a, state, scalars, 1.0 / 3.0, 2, 2 * HALO + CZ - 2, to_buffer(stage_b))
        between(1)
        section(stage_b, state, scalars, 0.5, 3, 2 * HALO + CZ - 3, to_buffer(stage_a))
        between(2)
        section(stage_a, state, scalars, 1.0, HALO, HALO + CZ, finish)
        between(3)

    halo_copies = []

    def pass_halos(field):
        for i in range(PEERS):
            second_copies[field * PEERS + i].wait_recv()
        for way, (neighbour, start, to) in enumerate(((below, HALO, HALO + CZ), (above, CZ, 0))):
            copy = pltpu.make_async_remote_copy(
                src_ref=lost.at[field, pl.ds(start, HALO)],
                dst_ref=lost.at[field, pl.ds(to, HALO)],
                send_sem=halo_send.at[field, way],
                recv_sem=halo_recv.at[field, way],
                device_id={"slab": neighbour},
                device_id_type=MESH,
            )
            copy.start()
            halo_copies.append(copy)

    live_in.wait()
    for copy in live_copies:
        copy.wait_recv()
    run_sections(live, stencil(levels_ref, 1), to_advanced, pass_halos)
    pass_halos(4)
    lost_scalars = stencil(levels_ref, 0)
    for copy in halo_copies:
        copy.wait_recv()
    run_sections(lost, lost_scalars, to_recovered, lambda step: None)

    recovered_out = pltpu.make_async_copy(recovered, recovered_ref, local_sem.at[0])
    recovered_out.start()

    third_copies = []
    for field in range(FIELDS):
        for i, peer in enumerate(peers):
            copy = pltpu.make_async_remote_copy(
                src_ref=weighted.at[peer, field],
                dst_ref=arrived.at[field, i],
                send_sem=send3.at[field, i],
                recv_sem=recv3.at[field, i],
                device_id={"buddy": peer},
                device_id_type=MESH,
            )
            copy.start()
            third_copies.append(copy)

    for field in range(FIELDS):
        total[field, 16] = jnp.zeros((2, CX), jnp.float32)
    fourth_copies = []
    for field in range(FIELDS):
        summed = weighted[me, field]
        for i in range(PEERS):
            third_copies[field * PEERS + i].wait_recv()
            summed = summed + arrived[field, i]
        for tile in range(16):
            total[field, tile] = summed[2 * tile : 2 * tile + 2]
        for i, peer in enumerate(peers):
            for rank in range(4):
                chosen[field, i, pl.ds(rank * 2, 2), :] = total[field, tiles_ref[peer * 4 + rank]]
            copy = pltpu.make_async_remote_copy(
                src_ref=chosen.at[field, i],
                dst_ref=combined_ref.at[field, me],
                send_sem=send4.at[field, i],
                recv_sem=recv4.at[field, i],
                device_id={"buddy": peer},
                device_id_type=MESH,
            )
            copy.start()
            fourth_copies.append(copy)
        for rank in range(4):
            combined_ref[field, me, pl.ds(rank * 2, 2), :] = total[field, tiles_ref[me * 4 + rank]]

    for copy in fourth_copies:
        copy.wait()
    for copy in first_copies + second_copies + third_copies + live_copies + halo_copies:
        copy.wait_send()
    recovered_out.wait()


def body(checkpoint, slot_block, live_state, levels, coefficients, tile_owner):
    ids = jnp.arange(64, dtype=jnp.int32)
    inverse = jnp.sum(jnp.where(slot_block.reshape(1, 64) == ids[:, None], ids[None, :], 0), axis=1)
    owners = tile_owner[0]
    order = jnp.arange(16, dtype=jnp.int32)
    ranks = jnp.sum(
        jnp.where((owners[None, :] == owners[:, None]) & (order[None, :] < order[:, None]), 1, 0), axis=1
    )
    slots = owners * 4 + ranks
    seats = jnp.arange(32, dtype=jnp.int32)
    tiles = 16 + jnp.sum(jnp.where(slots[None, :] == seats[:, None], order[None, :] - 16, 0), axis=1)
    smem = pl.BlockSpec(memory_space=pltpu.SMEM)
    away = pl.BlockSpec(memory_space=pl.ANY)
    dma = pltpu.SemaphoreType.DMA
    recovered, combined = pl.pallas_call(
        kernel,
        name="recover_and_combine",
        out_shape=(
            jax.ShapeDtypeStruct((FIELDS, CZ, CY, CX), jnp.float32),
            jax.ShapeDtypeStruct((FIELDS, CZ, 8, CX), jnp.float32),
        ),
        in_specs=[smem, smem, smem, smem, away, away],
        out_specs=(away, pl.BlockSpec(memory_space=pltpu.VMEM)),
        scratch_shapes=[
            *[pltpu.VMEM((64, 4, CX), jnp.float32) for _ in range(FIELDS)],
            pltpu.VMEM((FIELDS, PEERS, CY, CX), jnp.float32),
            pltpu.VMEM((FIELDS, CZ + 2 * HALO, CY, CX), jnp.float32),
            pltpu.VMEM((FIELDS, CZ + 2 * HALO, CY, CX), jnp.float32),
            pltpu.VMEM((FIELDS, CZ + 2 * HALO, CY, CX), jnp.float32),
            pltpu.VMEM((FIELDS, CZ + 2 * HALO, CY, CX), jnp.float32),
            pltpu.VMEM((CZ, FIELDS, CY, CX), jnp.float32),
            pltpu.VMEM((FIELDS, CZ, CY, CX), jnp.float32),
            pltpu.VMEM((CZ, FIELDS, CY, CX), jnp.float32),
            pltpu.VMEM((FIELDS, PEERS, CY, CX), jnp.float32),
            pltpu.VMEM((FIELDS, 17, 2, CX), jnp.float32),
            pltpu.VMEM((FIELDS, PEERS, 8, CX), jnp.float32),
            dma((1 + FIELDS,)),
            dma((FIELDS, PEERS)),
            dma((FIELDS, PEERS)),
            dma((FIELDS, PEERS)),
            dma((FIELDS, PEERS)),
            dma((FIELDS, PEERS)),
            dma((FIELDS, PEERS)),
            dma((FIELDS, PEERS)),
            dma((FIELDS, PEERS)),
            dma((FIELDS, 2)),
            dma((FIELDS, 2)),
            dma((2,)),
            dma((2,)),
        ],
        compiler_params=pltpu.CompilerParams(
            collective_id=0, has_side_effects=True, vmem_limit_bytes=48 << 20
        ),
    )(inverse, tiles, levels, coefficients, checkpoint, live_state)
    combined = combined.reshape(FIELDS, CZ, 4, 2, CX).transpose(2, 0, 1, 3, 4)
    return recovered[None], combined


def solution(mesh):
    return jax.shard_map(
        body,
        mesh=mesh,
        in_specs=(
            P("buddy", None, "slab", None, None),
            P(),
            P("buddy", None, "slab", None, None),
            P(None, "buddy", None),
            P(None, "buddy"),
            P("slab", None),
        ),
        out_specs=(P("buddy", None, "slab", None, None), P("buddy", None, "slab", None, None)),
        check_vma=False,
    )
```

```python
import functools

import jax
import jax.numpy as jnp
from jax import lax
from jax.experimental import pallas as pl
from jax.experimental.pallas import tpu as pltpu
from jax.sharding import PartitionSpec as P

MESH = pl.DeviceIdType.MESH
VELOCITY = (0.3, -0.2, 0.45)
FIELDS = 5
CZ = 8
CY = 32
CX = 256
HALO = 4
PEERS = 7
ALONG = (0, 1, 2)
ACROSS = (3, 4)
OFFSETS = ((2, 1), (2, 0), (1, 1), (3, 1), (0, 1), (1, 0), (3, 0))


def stencil(levels_ref, kind):
    inverse = []
    for axis in range(3):
        level = levels_ref[kind, 0, axis]
        inverse.append(jnp.where(level == 0, 1.0, jnp.where(level == 1, 2.0, 4.0)).astype(jnp.float32))
    denominator = (abs(VELOCITY[0]) + 1.0) * inverse[0] + (abs(VELOCITY[1]) + 1.0) * inverse[1]
    denominator = denominator + (abs(VELOCITY[2]) + 1.0) * inverse[2]
    step = jnp.max(1.0 / jnp.full((8, 128), denominator, jnp.float32))
    middle = -step * denominator
    sides = []
    for axis in range(3):
        scaled = step * inverse[axis]
        half = 0.5 * (abs(VELOCITY[axis]) + 1.0)
        sides.append(
            (
                scaled * (half - 0.5 * VELOCITY[axis]),
                scaled * (half + 0.5 * VELOCITY[axis]),
                scaled * -0.5,
            )
        )
    return middle, sides


def section(source, base, scalars, share, first, last, write):
    middle, sides = scalars
    middle = middle * share
    sides = [tuple(value * share for value in side) for side in sides]

    def one_layer(z, carry):
        def own_terms(field):
            q = source[field, z]
            out = base[field, z] + middle * q
            shifted = (
                (pltpu.roll(q, CX - 1, 1), pltpu.roll(q, 1, 1)),
                (pltpu.roll(q, CY - 1, 0), pltpu.roll(q, 1, 0)),
                (source[field, z + 1], source[field, z - 1]),
            )
            for (plus, minus), side in zip(shifted, sides):
                out = out + (side[0] * plus + side[1] * minus)
            return out, shifted

        pressure, around = own_terms(4)
        pushes = [side[2] * (plus - minus) for (plus, minus), side in zip(around, sides)]
        spread = None
        results = [None] * FIELDS
        for axis in range(3):
            out, around = own_terms(1 + axis)
            results[1 + axis] = out + pushes[axis]
            part = sides[axis][2] * (around[axis][0] - around[axis][1])
            spread = part if spread is None else spread + part
        results[4] = pressure + spread
        results[0] = own_terms(0)[0] + spread
        write(z, results)
        return carry

    lax.fori_loop(first, last, one_layer, 0)


def kernel(
    slots_ref,
    owners_ref,
    levels_ref,
    coefficients_ref,
    checkpoint_ref,
    live_ref,
    recovered_ref,
    combined_ref,
    lines_0,
    lines_1,
    lines_2,
    lines_3,
    lines_4,
    packed,
    lost,
    live,
    stage_a,
    stage_b,
    advanced,
    recovered,
    weighted,
    far_in,
    near_out,
    near_in,
    across_out,
    across_in,
    columns,
    total,
    chosen,
    tables,
    numbers,
    local_sem,
    send1,
    recv1,
    send2,
    recv2,
    send3,
    recv3,
    send4,
    recv4,
    wrap_send,
    wrap_recv,
    halo_send,
    halo_recv,
    live_send,
    live_recv,
):
    lines = (lines_0, lines_1, lines_2, lines_3, lines_4)
    slab = lax.axis_index("slab")
    me = lax.axis_index("buddy")
    slabs = lax.axis_size("slab")
    row, half = me // 2, me % 2
    above = (slab + 1) % slabs
    below = (slab + slabs - 1) % slabs

    def at(offset):
        return ((row + offset[0]) % 4) * 2 + (half + offset[1]) % 2

    peers = [at(offset) for offset in OFFSETS]
    sources = [at(((4 - offset[0]) % 4, offset[1])) for offset in OFFSETS]

    wraps = ((slab % 8 == 0, below, 0, HALO + CZ), (slab % 8 == 7, above, HALO, -HALO))

    barrier = pltpu.get_barrier_semaphore()
    for peer in peers:
        pl.semaphore_signal(barrier, inc=1, device_id={"buddy": peer}, device_id_type=MESH)
    for neighbour in (below, above):
        pl.semaphore_signal(barrier, inc=1, device_id={"slab": neighbour}, device_id_type=MESH)
    for wrap, neighbour, _, _ in wraps:

        @pl.when(wrap)
        def _():
            for peer in peers:
                pl.semaphore_signal(
                    barrier, inc=1, device_id={"slab": neighbour, "buddy": peer}, device_id_type=MESH
                )

    live_in = pltpu.make_async_copy(live_ref.at[0], live.at[:, pl.ds(HALO, CZ)], local_sem.at[0])
    live_in.start()
    own_copies = []
    for field in range(FIELDS):
        copy = pltpu.make_async_copy(
            checkpoint_ref.at[:, field, me], lines[field].at[pl.ds(me * 8, 8)], local_sem.at[1 + field]
        )
        copy.start()
        own_copies.append(copy)

    crossing = jnp.logical_or(wraps[0][0], wraps[1][0])
    pl.semaphore_wait(barrier, jnp.where(crossing, 2 * PEERS + 2, PEERS + 2))

    first_copies = []
    for field in range(FIELDS):
        for i, peer in enumerate(peers):
            copy = pltpu.make_async_remote_copy(
                src_ref=checkpoint_ref.at[:, field, peer],
                dst_ref=lines[field].at[pl.ds(me * 8, 8)],
                send_sem=send1.at[field, i],
                recv_sem=recv1.at[field, i],
                device_id={"buddy": peer},
                device_id_type=MESH,
            )
            copy.start()
            first_copies.append(copy)
    live_copies = []
    for way, (neighbour, start, to) in enumerate(((below, 0, HALO + CZ), (above, CZ - HALO, 0))):
        copy = pltpu.make_async_remote_copy(
            src_ref=live_ref.at[0, :, pl.ds(start, HALO)],
            dst_ref=live.at[:, pl.ds(to, HALO)],
            send_sem=live_send.at[way],
            recv_sem=live_recv.at[way],
            device_id={"slab": neighbour},
            device_id_type=MESH,
        )
        copy.start()
        live_copies.append(copy)

    lanes = lax.broadcasted_iota(jnp.int32, (8, 128), 1)
    held_in = jnp.zeros((8, 128), jnp.int32)
    for slot in range(64):
        held_in = jnp.where(lanes == slots_ref[slot // 8, slot % 8], slot, held_in)
    tables[0:8] = held_in
    owners = [owners_ref[0, tile] for tile in range(16)]
    seated = jnp.full((8, 128), 16, jnp.int32)
    for tile in range(16):
        rank = sum([(owners[before] == owners[tile]).astype(jnp.int32) for before in range(tile)], 0)
        seated = jnp.where(lanes == owners[tile] * 4 + rank, tile, seated)
    tables[8:16] = seated
    tables_in = pltpu.make_async_copy(tables, numbers, local_sem.at[1 + FIELDS])
    tables_in.start()

    tables_in.wait()
    second_copies = []

    def pass_layers(field):
        own_copies[field].wait()
        for i in range(PEERS):
            first_copies[field * PEERS + i].wait_recv()
        for i, peer in enumerate(peers):
            for block in range(8):
                packed[field, i, pl.ds(block * 4, 4), :] = lines[field][numbers[0, peer * 8 + block]]
            copy = pltpu.make_async_remote_copy(
                src_ref=packed.at[field, i],
                dst_ref=lost.at[field, HALO + me],
                send_sem=send2.at[field, i],
                recv_sem=recv2.at[field, i],
                device_id={"buddy": peer},
                device_id_type=MESH,
            )
            copy.start()
            second_copies.append(copy)
        for block in range(8):
            packed[field, PEERS, pl.ds(block * 4, 4), :] = lines[field][numbers[0, me * 8 + block]]
        lost[field, HALO + me] = packed[field, PEERS]
        for i in range(PEERS + 1):
            for way in range(2):
                wrapped(field, i, way, "start")

    def wrapped(field, i, way, action):
        wrap, neighbour, first, to = wraps[way]
        peer = me if i == PEERS else peers[i]
        layer = me - first

        @pl.when(jnp.logical_and(wrap, jnp.logical_and(layer >= 0, layer < HALO)))
        def _():
            copy = pltpu.make_async_remote_copy(
                src_ref=packed.at[field, i],
                dst_ref=lost.at[field, me + to],
                send_sem=wrap_send.at[field, i],
                recv_sem=wrap_recv.at[field, way, layer],
                device_id={"slab": neighbour, "buddy": peer},
                device_id_type=MESH,
            )
            copy.start() if action == "start" else copy.wait_send()

    def to_buffer(buffer):
        def write(z, results):
            for field in range(FIELDS):
                buffer[field, z] = results[field]

        return write

    def to_advanced(z, results):
        for field in range(FIELDS):
            advanced[z - HALO, field] = results[field]

    share = coefficients_ref[0, 0]
    live_share = coefficients_ref[0, 1]

    def to_recovered(z, results):
        for field in range(FIELDS):
            recovered[field, z - HALO] = results[field]
            weighted[(z - HALO) // 2, (z - HALO) % 2, field] = share * results[field] + live_share * advanced[z - HALO, field]

    def run_sections(state, scalars, finish, between):
        section(state, state, scalars, 0.25, 1, 2 * HALO + CZ - 1, to_buffer(stage_a))
        between(0)
        section(stage_a, state, scalars, 1.0 / 3.0, 2, 2 * HALO + CZ - 2, to_buffer(stage_b))
        between(1)
        section(stage_b, state, scalars, 0.5, 3, 2 * HALO + CZ - 3, to_buffer(stage_a))
        between(2)
        section(stage_a, state, scalars, 1.0, HALO, HALO + CZ, finish)
        between(3)

    def pass_halos(field):
        for i in range(PEERS):
            second_copies[field * PEERS + i].wait_recv()
        for way in range(2):
            halo(field, way, "start")

    def halo(field, way, action):
        wrap, neighbour, first, to = wraps[way]

        def copy():
            return pltpu.make_async_remote_copy(
                src_ref=lost.at[field, pl.ds(HALO + first, HALO)],
                dst_ref=lost.at[field, pl.ds(first + to, HALO)],
                send_sem=halo_send.at[field, way],
                recv_sem=halo_recv.at[field, way],
                device_id={"slab": neighbour},
                device_id_type=MESH,
            )

        if action == "start" or action == "sent":

            @pl.when(jnp.logical_not(wrap))
            def _():
                copy().start() if action == "start" else copy().wait_send()

        else:
            far = wraps[1 - way][0]

            @pl.when(jnp.logical_not(far))
            def _():
                copy().wait_recv()

            @pl.when(far)
            def _():
                for layer in range(HALO):
                    pltpu.make_async_remote_copy(
                        src_ref=packed.at[field, 0],
                        dst_ref=lost.at[field, first + to + layer],
                        send_sem=wrap_send.at[field, 0],
                        recv_sem=wrap_recv.at[field, way, layer],
                        device_id={"slab": neighbour},
                        device_id_type=MESH,
                    ).wait_recv()

    def between(step):
        if step != 1:
            pass_halos((2, None, 3, 4)[step])

    pass_layers(0)
    pass_layers(1)
    pass_layers(2)
    pass_halos(0)
    pass_layers(3)
    pass_halos(1)
    pass_layers(4)
    live_in.wait()
    for copy in live_copies:
        copy.wait_recv()
    run_sections(live, stencil(levels_ref, 1), to_advanced, between)
    lost_scalars = stencil(levels_ref, 0)
    for field in range(FIELDS):
        for way in range(2):
            halo(field, way, "received")
    run_sections(lost, lost_scalars, to_recovered, lambda step: None)

    recovered_out = pltpu.make_async_copy(recovered, recovered_ref, local_sem.at[0])
    recovered_out.start()

    signs = (1, 3)
    sides = [((row + sign) % 4) * 2 + half for sign in signs]
    across = row * 2 + 1 - half
    third_copies = {}

    def send(field, message, source, target, peer):
        copy = pltpu.make_async_remote_copy(
            src_ref=source,
            dst_ref=target,
            send_sem=send3.at[field, message],
            recv_sem=recv3.at[field, message],
            device_id={"buddy": peer},
            device_id_type=MESH,
        )
        copy.start()
        third_copies[field, message] = copy

    def rows(way):
        return pl.ds(way * (CY // 2), CY // 2)

    def start_along(field):
        far = (row + 2) % 4
        for way, sign in enumerate(signs):
            near = (row + sign) % 4
            send(field, way, weighted.at[far, way, field], far_in.at[way, field], sides[way])
            send(field, 2 + way, weighted.at[near, 1 - way, field], near_in.at[way, field, 1 - way], sides[way])

    def pass_along(field):
        for way, sign in enumerate(signs):
            near = (row + sign) % 4
            third_copies[field, way].wait_recv()
            near_out[way, field] = far_in[way, field] + weighted[near, way, field]
            send(field, 4 + way, near_out.at[way, field], near_in.at[way, field, way], sides[way])

    def finish_along(field):
        for message in range(2, 6):
            third_copies[field, message].wait_recv()

        def column(layer):
            return weighted[row, layer, field] + (near_in[0, field, layer] + near_in[1, field, layer])

        across_out[field] = column(1 - half)
        columns[field, 0] = column(half)
        send(field, 6, across_out.at[field], across_in.at[field, 0], across)

    def start_across(field):
        send(field, 6, weighted.at[:, 1 - half, field], across_in.at[field], across)

    def turn_across(field):
        third_copies[field, 6].wait_recv()
        for column in range(4):
            columns[field, column] = weighted[column, half, field] + across_in[field, column]
        far = (row + 2) % 4
        for way, sign in enumerate(signs):
            near = (row + sign) % 4
            send(field, way, columns.at[field, far, rows(way)], far_in.at[way, field, rows(way)], sides[way])
            send(
                field,
                2 + way,
                columns.at[field, near, rows(1 - way)],
                near_in.at[way, field, 0, rows(1 - way)],
                sides[way],
            )

    def pass_across(field):
        for way, sign in enumerate(signs):
            near = (row + sign) % 4
            third_copies[field, way].wait_recv()
            near_out[way, field, rows(way)] = far_in[way, field, rows(way)] + columns[field, near, rows(way)]
            send(
                field,
                4 + way,
                near_out.at[way, field, rows(way)],
                near_in.at[way, field, 0, rows(way)],
                sides[way],
            )

    def whole_along(field):
        third_copies[field, 6].wait_recv()
        return columns[field, 0] + across_in[field, 0]

    def whole_across(field):
        for message in range(2, 6):
            third_copies[field, message].wait_recv()
        return columns[field, row] + (near_in[0, field, 0] + near_in[1, field, 0])

    for step, fields in (
        (start_across, ACROSS),
        (start_along, ALONG),
        (pass_along, ALONG),
        (turn_across, ACROSS),
        (finish_along, ALONG),
        (pass_across, ACROSS),
    ):
        for field in fields:
            step(field)

    for field in range(FIELDS):
        total[field, 16] = jnp.zeros((2, CX), jnp.float32)
    fourth_copies = []
    for field in ALONG + ACROSS:
        summed = whole_along(field) if field in ALONG else whole_across(field)
        for tile in range(16):
            total[field, tile] = summed[2 * tile : 2 * tile + 2]
        for i, peer in enumerate(peers):
            for rank in range(4):
                chosen[field, i, rank] = total[field, numbers[8, peer * 4 + rank]]
            copy = pltpu.make_async_remote_copy(
                src_ref=chosen.at[field, i],
                dst_ref=combined_ref.at[:, field, me],
                send_sem=send4.at[field, i],
                recv_sem=recv4.at[field, i],
                device_id={"buddy": peer},
                device_id_type=MESH,
            )
            copy.start()
            fourth_copies.append(copy)
        for rank in range(4):
            combined_ref[rank, field, me] = total[field, numbers[8, me * 4 + rank]]

    recovered_out.wait()
    for copy in fourth_copies:
        copy.wait()
    for copy in first_copies + second_copies + list(third_copies.values()) + live_copies:
        copy.wait_send()
    for field in range(FIELDS):
        for way in range(2):
            halo(field, way, "sent")
            for i in range(PEERS + 1):
                wrapped(field, i, way, "sent")


def hand_over(recovered, combined):
    def copies(recovered_in, combined_in, recovered_out, combined_out, fields, tiles, sem_in, sem_out):
        pairs = [
            (recovered_in.at[0, field], fields.at[field], recovered_out.at[0, field]) for field in range(FIELDS)
        ] + [(combined_in, tiles, combined_out)]
        first = [
            pltpu.make_async_copy(pair[0], pair[1], sem_in.at[i]) for i, pair in enumerate(pairs)
        ]
        second = [
            pltpu.make_async_copy(pair[1], pair[2], sem_out.at[i]) for i, pair in enumerate(pairs)
        ]
        for copy in first:
            copy.start()
        for before, after in zip(first, second):
            before.wait()
            after.start()
        for copy in second:
            copy.wait()

    away = pl.BlockSpec(memory_space=pltpu.HBM)
    return pl.pallas_call(
        copies,
        name="hand_over",
        out_shape=(
            jax.ShapeDtypeStruct(recovered.shape, recovered.dtype),
            jax.ShapeDtypeStruct(combined.shape, combined.dtype),
        ),
        in_specs=[away, away],
        out_specs=(away, away),
        scratch_shapes=[
            pltpu.VMEM(recovered.shape[1:], jnp.float32),
            pltpu.VMEM(combined.shape, jnp.float32),
            pltpu.SemaphoreType.DMA((FIELDS + 1,)),
            pltpu.SemaphoreType.DMA((FIELDS + 1,)),
        ],
        compiler_params=pltpu.CompilerParams(vmem_limit_bytes=63 << 20),
    )(recovered, combined)


def body(checkpoint, slot_block, live_state, levels, coefficients, tile_owner):
    smem = pl.BlockSpec(memory_space=pltpu.SMEM)
    away = pl.BlockSpec(memory_space=pltpu.HBM)
    dma = pltpu.SemaphoreType.DMA
    recovered, combined = pl.pallas_call(
        kernel,
        name="recover_and_combine",
        out_shape=(
            jax.ShapeDtypeStruct((FIELDS, CZ, CY, CX), jnp.float32),
            jax.ShapeDtypeStruct((4, FIELDS, CZ, 2, CX), jnp.float32),
        ),
        in_specs=[smem, smem, smem, smem, away, away],
        out_specs=(away, pl.BlockSpec(memory_space=pltpu.VMEM)),
        scratch_shapes=[
            *[pltpu.VMEM((64, 4, CX), jnp.float32) for _ in range(FIELDS)],
            pltpu.VMEM((FIELDS, PEERS + 1, CY, CX), jnp.float32),
            pltpu.VMEM((FIELDS, CZ + 2 * HALO, CY, CX), jnp.float32),
            pltpu.VMEM((FIELDS, CZ + 2 * HALO, CY, CX), jnp.float32),
            pltpu.VMEM((FIELDS, CZ + 2 * HALO, CY, CX), jnp.float32),
            pltpu.VMEM((FIELDS, CZ + 2 * HALO, CY, CX), jnp.float32),
            pltpu.VMEM((CZ, FIELDS, CY, CX), jnp.float32),
            pltpu.VMEM((FIELDS, CZ, CY, CX), jnp.float32),
            pltpu.VMEM((4, 2, FIELDS, CY, CX), jnp.float32),
            pltpu.VMEM((2, FIELDS, CY, CX), jnp.float32),
            pltpu.VMEM((2, FIELDS, CY, CX), jnp.float32),
            pltpu.VMEM((2, FIELDS, 2, CY, CX), jnp.float32),
            pltpu.VMEM((FIELDS, CY, CX), jnp.float32),
            pltpu.VMEM((FIELDS, 4, CY, CX), jnp.float32),
            pltpu.VMEM((FIELDS, 4, CY, CX), jnp.float32),
            pltpu.VMEM((FIELDS, 17, 2, CX), jnp.float32),
            pltpu.VMEM((FIELDS, PEERS, 4, 2, CX), jnp.float32),
            pltpu.VMEM((16, 128), jnp.int32),
            pltpu.SMEM((16, 128), jnp.int32),
            dma((2 + FIELDS,)),
            dma((FIELDS, PEERS)),
            dma((FIELDS, PEERS)),
            dma((FIELDS, PEERS)),
            dma((FIELDS, PEERS)),
            dma((FIELDS, PEERS)),
            dma((FIELDS, PEERS)),
            dma((FIELDS, PEERS)),
            dma((FIELDS, PEERS)),
            dma((FIELDS, PEERS + 1)),
            dma((FIELDS, 2, HALO)),
            dma((FIELDS, 2)),
            dma((FIELDS, 2)),
            dma((2,)),
            dma((2,)),
        ],
        compiler_params=pltpu.CompilerParams(
            collective_id=0, has_side_effects=True, vmem_limit_bytes=63 << 20
        ),
    )(slot_block, tile_owner, levels, coefficients.reshape(1, 2), checkpoint, live_state)
    return hand_over(recovered[None], combined)


def solution(mesh):
    return jax.shard_map(
        body,
        mesh=mesh,
        in_specs=(
            P("buddy", None, "slab", None, None),
            P(),
            P("buddy", None, "slab", None, None),
            P(None, "buddy", None),
            P(None, "buddy"),
            P("slab", None),
        ),
        out_specs=(P("buddy", None, "slab", None, None), P("buddy", None, "slab", None, None)),
        check_vma=False,
    )
```

```python
import functools

import jax
import jax.numpy as jnp
from jax import lax
from jax.experimental import pallas as pl
from jax.experimental.pallas import tpu as pltpu
from jax.sharding import PartitionSpec as P

MESH = pl.DeviceIdType.MESH
VELOCITY = (0.3, -0.2, 0.45)
FIELDS = 5
CZ = 8
CY = 32
CX = 256
HALO = 4
PEERS = 7
OFFSETS = ((2, 1), (2, 0), (1, 1), (3, 1), (0, 1), (1, 0), (3, 0))


def stencil(levels_ref, kind):
    inverse = []
    for axis in range(3):
        level = levels_ref[kind, 0, axis]
        inverse.append(jnp.where(level == 0, 1.0, jnp.where(level == 1, 2.0, 4.0)).astype(jnp.float32))
    denominator = (abs(VELOCITY[0]) + 1.0) * inverse[0] + (abs(VELOCITY[1]) + 1.0) * inverse[1]
    denominator = denominator + (abs(VELOCITY[2]) + 1.0) * inverse[2]
    step = jnp.max(1.0 / jnp.full((8, 128), denominator, jnp.float32))
    middle = -step * denominator
    sides = []
    for axis in range(3):
        scaled = step * inverse[axis]
        half = 0.5 * (abs(VELOCITY[axis]) + 1.0)
        sides.append(
            (
                scaled * (half - 0.5 * VELOCITY[axis]),
                scaled * (half + 0.5 * VELOCITY[axis]),
                scaled * -0.5,
            )
        )
    return middle, sides


def section(source, base, scalars, share, first, last, write):
    middle, sides = scalars
    middle = middle * share
    sides = [tuple(value * share for value in side) for side in sides]

    def one_layer(z, carry):
        def own_terms(field):
            q = source[field, z]
            out = base[field, z] + middle * q
            shifted = (
                (pltpu.roll(q, CX - 1, 1), pltpu.roll(q, 1, 1)),
                (pltpu.roll(q, CY - 1, 0), pltpu.roll(q, 1, 0)),
                (source[field, z + 1], source[field, z - 1]),
            )
            for (plus, minus), side in zip(shifted, sides):
                out = out + (side[0] * plus + side[1] * minus)
            return out, shifted

        pressure, around = own_terms(4)
        pushes = [side[2] * (plus - minus) for (plus, minus), side in zip(around, sides)]
        spread = None
        results = [None] * FIELDS
        for axis in range(3):
            out, around = own_terms(1 + axis)
            results[1 + axis] = out + pushes[axis]
            part = sides[axis][2] * (around[axis][0] - around[axis][1])
            spread = part if spread is None else spread + part
        results[4] = pressure + spread
        results[0] = own_terms(0)[0] + spread
        write(z, results)
        return carry

    lax.fori_loop(first, last, one_layer, 0)


def kernel(
    slots_ref,
    owners_ref,
    levels_ref,
    coefficients_ref,
    checkpoint_ref,
    live_ref,
    recovered_ref,
    combined_ref,
    lines_0,
    lines_1,
    lines_2,
    lines_3,
    lines_4,
    packed,
    lost,
    live,
    stage_a,
    stage_b,
    live_a,
    live_b,
    advanced,
    recovered,
    weighted,
    arrived,
    total,
    chosen,
    tables,
    numbers,
    local_sem,
    send1,
    recv1,
    send2,
    recv2,
    send3,
    recv3,
    send4,
    recv4,
    wrap_send,
    wrap_recv,
    halo_send,
    halo_recv,
    live_send,
    live_recv,
):
    lines = (lines_0, lines_1, lines_2, lines_3, lines_4)
    slab = lax.axis_index("slab")
    me = lax.axis_index("buddy")
    slabs = lax.axis_size("slab")
    row, half = me // 2, me % 2
    above = (slab + 1) % slabs
    below = (slab + slabs - 1) % slabs

    def at(offset):
        return ((row + offset[0]) % 4) * 2 + (half + offset[1]) % 2

    peers = [at(offset) for offset in OFFSETS]
    sources = [at(((4 - offset[0]) % 4, offset[1])) for offset in OFFSETS]

    wraps = ((slab % 8 == 0, below, 0, HALO + CZ), (slab % 8 == 7, above, HALO, -HALO))

    barrier = pltpu.get_barrier_semaphore()
    for peer in peers:
        pl.semaphore_signal(barrier, inc=1, device_id={"buddy": peer}, device_id_type=MESH)
    for neighbour in (below, above):
        pl.semaphore_signal(barrier, inc=1, device_id={"slab": neighbour}, device_id_type=MESH)
    for wrap, neighbour, _, _ in wraps:

        @pl.when(wrap)
        def _():
            for peer in peers:
                pl.semaphore_signal(
                    barrier, inc=1, device_id={"slab": neighbour, "buddy": peer}, device_id_type=MESH
                )

    live_in = pltpu.make_async_copy(live_ref.at[0], live.at[:, pl.ds(HALO, CZ)], local_sem.at[0])
    live_in.start()
    own_copies = []
    for field in range(FIELDS):
        copy = pltpu.make_async_copy(
            checkpoint_ref.at[:, field, me], lines[field].at[pl.ds(me * 8, 8)], local_sem.at[1 + field]
        )
        copy.start()
        own_copies.append(copy)

    crossing = jnp.logical_or(wraps[0][0], wraps[1][0])
    pl.semaphore_wait(barrier, jnp.where(crossing, 2 * PEERS + 2, PEERS + 2))

    first_copies = []
    for field in range(FIELDS):
        for i, peer in enumerate(peers):
            copy = pltpu.make_async_remote_copy(
                src_ref=checkpoint_ref.at[:, field, peer],
                dst_ref=lines[field].at[pl.ds(me * 8, 8)],
                send_sem=send1.at[field, i],
                recv_sem=recv1.at[field, i],
                device_id={"buddy": peer},
                device_id_type=MESH,
            )
            copy.start()
            first_copies.append(copy)

    def live_copy(way):
        _, neighbour, first, to = wraps[way]
        return pltpu.make_async_remote_copy(
            src_ref=live_ref.at[0, :, pl.ds(first, HALO)],
            dst_ref=live.at[:, pl.ds(first + to, HALO)],
            send_sem=live_send.at[way],
            recv_sem=live_recv.at[way],
            device_id={"slab": neighbour},
            device_id_type=MESH,
        )

    def start_live(across_the_slice):
        for way in range(2):
            wrap = wraps[way][0]

            @pl.when(wrap if across_the_slice else jnp.logical_not(wrap))
            def _():
                live_copy(way).start()

    start_live(False)

    lanes = lax.broadcasted_iota(jnp.int32, (8, 128), 1)
    held_in = jnp.zeros((8, 128), jnp.int32)
    for slot in range(64):
        held_in = jnp.where(lanes == slots_ref[slot // 8, slot % 8], slot, held_in)
    tables[0:8] = held_in
    owners = [owners_ref[0, tile] for tile in range(16)]
    seated = jnp.full((8, 128), 16, jnp.int32)
    for tile in range(16):
        rank = sum([(owners[before] == owners[tile]).astype(jnp.int32) for before in range(tile)], 0)
        seated = jnp.where(lanes == owners[tile] * 4 + rank, tile, seated)
    tables[8:16] = seated
    tables_in = pltpu.make_async_copy(tables, numbers, local_sem.at[1 + FIELDS])
    tables_in.start()

    tables_in.wait()
    second_copies = []

    def pass_layers(field):
        own_copies[field].wait()
        for i in range(PEERS):
            first_copies[field * PEERS + i].wait_recv()
        for i, peer in enumerate(peers):
            for block in range(8):
                packed[field, i, pl.ds(block * 4, 4), :] = lines[field][numbers[0, peer * 8 + block]]
            copy = pltpu.make_async_remote_copy(
                src_ref=packed.at[field, i],
                dst_ref=lost.at[field, HALO + me],
                send_sem=send2.at[field, i],
                recv_sem=recv2.at[field, i],
                device_id={"buddy": peer},
                device_id_type=MESH,
            )
            copy.start()
            second_copies.append(copy)
        for block in range(8):
            packed[field, PEERS, pl.ds(block * 4, 4), :] = lines[field][numbers[0, me * 8 + block]]
        lost[field, HALO + me] = packed[field, PEERS]
        for i in range(PEERS + 1):
            for way in range(2):
                wrapped(field, i, way, "start")

    def wrapped(field, i, way, action):
        wrap, neighbour, first, to = wraps[way]
        peer = me if i == PEERS else peers[i]
        layer = me - first

        @pl.when(jnp.logical_and(wrap, jnp.logical_and(layer >= 0, layer < HALO)))
        def _():
            copy = pltpu.make_async_remote_copy(
                src_ref=packed.at[field, i],
                dst_ref=lost.at[field, me + to],
                send_sem=wrap_send.at[field, i],
                recv_sem=wrap_recv.at[field, way, layer],
                device_id={"slab": neighbour, "buddy": peer},
                device_id_type=MESH,
            )
            copy.start() if action == "start" else copy.wait_send()

    def to_buffer(buffer):
        def write(z, results):
            for field in range(FIELDS):
                buffer[field, z] = results[field]

        return write

    def to_advanced(z, results):
        for field in range(FIELDS):
            advanced[z - HALO, field] = results[field]

    share = coefficients_ref[0, 0]
    live_share = coefficients_ref[0, 1]

    def to_recovered(z, results):
        for field in range(FIELDS):
            recovered[field, z - HALO] = results[field]
            weighted[(z - HALO) // 2, (z - HALO) % 2, field] = share * results[field] + live_share * advanced[z - HALO, field]

    def to_weighted(z, results):
        for field in range(FIELDS):
            weighted[(z - HALO) // 2, (z - HALO) % 2, field] = (
                share * recovered[field, z - HALO] + live_share * results[field]
            )

    def run_sections(state, scalars, finish):
        section(state, state, scalars, 0.25, 1, 2 * HALO + CZ - 1, to_buffer(stage_a))
        section(stage_a, state, scalars, 1.0 / 3.0, 2, 2 * HALO + CZ - 2, to_buffer(stage_b))
        section(stage_b, state, scalars, 0.5, 3, 2 * HALO + CZ - 3, to_buffer(stage_a))
        section(stage_a, state, scalars, 1.0, HALO, HALO + CZ, finish)

    def pass_halos(field):
        for i in range(PEERS):
            second_copies[field * PEERS + i].wait_recv()
        for way in range(2):
            halo(field, way, "start")

    def halo(field, way, action):
        wrap, neighbour, first, to = wraps[way]

        def copy():
            return pltpu.make_async_remote_copy(
                src_ref=lost.at[field, pl.ds(HALO + first, HALO)],
                dst_ref=lost.at[field, pl.ds(first + to, HALO)],
                send_sem=halo_send.at[field, way],
                recv_sem=halo_recv.at[field, way],
                device_id={"slab": neighbour},
                device_id_type=MESH,
            )

        if action == "start" or action == "sent":

            @pl.when(jnp.logical_not(wrap))
            def _():
                copy().start() if action == "start" else copy().wait_send()

        else:
            far = wraps[1 - way][0]

            @pl.when(jnp.logical_not(far))
            def _():
                copy().wait_recv()

            @pl.when(far)
            def _():
                for layer in range(HALO):
                    pltpu.make_async_remote_copy(
                        src_ref=packed.at[field, 0],
                        dst_ref=lost.at[field, first + to + layer],
                        send_sem=wrap_send.at[field, 0],
                        recv_sem=wrap_recv.at[field, way, layer],
                        device_id={"slab": neighbour},
                        device_id_type=MESH,
                    ).wait_recv()

    live_scalars = stencil(levels_ref, 1)
    lost_scalars = stencil(levels_ref, 0)
    last = 2 * HALO + CZ

    def live_section(step, spans, finish):
        source, share_of_step, write = (
            (live, 0.25, to_buffer(live_a)),
            (live_a, 1.0 / 3.0, to_buffer(live_b)),
            (live_b, 0.5, to_buffer(live_a)),
            (live_a, 1.0, finish),
        )[step]
        for first, end in spans:
            section(source, live, live_scalars, share_of_step, first, end, write)

    def early_live(step):
        @pl.when(jnp.logical_not(crossing))
        def _():
            if step == 0:
                for way in range(2):
                    live_copy(way).wait_recv()
            live_section(step, ((1 + step, last - 1 - step),), to_advanced)

        if step < 3:

            @pl.when(crossing)
            def _():
                live_section(step, ((HALO + 1 + step, HALO + CZ - 1 - step),), None)

    def late_live():
        @pl.when(crossing)
        def _():
            for way in range(2):
                live_copy(way).wait_recv()
            for step in range(3):
                live_section(
                    step,
                    ((1 + step, HALO + 1 + step), (HALO + CZ - 1 - step, last - 1 - step)),
                    None,
                )
            live_section(3, ((HALO, HALO + CZ),), to_weighted)

    pass_layers(0)
    pass_layers(1)
    pass_layers(2)
    pass_halos(0)
    pass_layers(3)
    pass_halos(1)
    pass_layers(4)
    live_in.wait()
    early_live(0)
    pass_halos(2)
    early_live(1)
    early_live(2)
    pass_halos(3)
    early_live(3)
    pass_halos(4)
    start_live(True)
    for field in range(FIELDS):
        for way in range(2):
            halo(field, way, "received")
    run_sections(lost, lost_scalars, to_recovered)
    late_live()

    recovered_out = pltpu.make_async_copy(recovered, recovered_ref, local_sem.at[0])
    recovered_out.start()

    third_copies = {}
    for field in range(FIELDS):
        for i, peer in enumerate(peers):
            copy = pltpu.make_async_remote_copy(
                src_ref=weighted.at[peer // 2, peer % 2, field],
                dst_ref=arrived.at[field, i],
                send_sem=send3.at[field, i],
                recv_sem=recv3.at[field, i],
                device_id={"buddy": peer},
                device_id_type=MESH,
            )
            copy.start()
            third_copies[field, i] = copy

    for field in range(FIELDS):
        total[field, 16] = jnp.zeros((2, CX), jnp.float32)
    fourth_copies = []
    for field in range(FIELDS):
        summed = weighted[row, half, field]
        for i in range(PEERS):
            third_copies[field, i].wait_recv()
            summed = summed + arrived[field, i]
        for tile in range(16):
            total[field, tile] = summed[2 * tile : 2 * tile + 2]
        for i, peer in enumerate(peers):
            for rank in range(4):
                chosen[field, i, rank] = total[field, numbers[8, peer * 4 + rank]]
            copy = pltpu.make_async_remote_copy(
                src_ref=chosen.at[field, i],
                dst_ref=combined_ref.at[:, field, me],
                send_sem=send4.at[field, i],
                recv_sem=recv4.at[field, i],
                device_id={"buddy": peer},
                device_id_type=MESH,
            )
            copy.start()
            fourth_copies.append(copy)
        for rank in range(4):
            combined_ref[rank, field, me] = total[field, numbers[8, me * 4 + rank]]

    recovered_out.wait()
    for copy in fourth_copies:
        copy.wait()
    for copy in first_copies + second_copies + list(third_copies.values()):
        copy.wait_send()
    for way in range(2):
        live_copy(way).wait_send()
    for field in range(FIELDS):
        for way in range(2):
            halo(field, way, "sent")
            for i in range(PEERS + 1):
                wrapped(field, i, way, "sent")


def hand_over(recovered, combined):
    def copies(recovered_in, combined_in, recovered_out, combined_out, fields, tiles, sem_in, sem_out):
        pairs = [
            (recovered_in.at[0, field], fields.at[field], recovered_out.at[0, field]) for field in range(FIELDS)
        ] + [(combined_in, tiles, combined_out)]
        first = [
            pltpu.make_async_copy(pair[0], pair[1], sem_in.at[i]) for i, pair in enumerate(pairs)
        ]
        second = [
            pltpu.make_async_copy(pair[1], pair[2], sem_out.at[i]) for i, pair in enumerate(pairs)
        ]
        for copy in first:
            copy.start()
        for before, after in zip(first, second):
            before.wait()
            after.start()
        for copy in second:
            copy.wait()

    away = pl.BlockSpec(memory_space=pltpu.HBM)
    return pl.pallas_call(
        copies,
        name="hand_over",
        out_shape=(
            jax.ShapeDtypeStruct(recovered.shape, recovered.dtype),
            jax.ShapeDtypeStruct(combined.shape, combined.dtype),
        ),
        in_specs=[away, away],
        out_specs=(away, away),
        scratch_shapes=[
            pltpu.VMEM(recovered.shape[1:], jnp.float32),
            pltpu.VMEM(combined.shape, jnp.float32),
            pltpu.SemaphoreType.DMA((FIELDS + 1,)),
            pltpu.SemaphoreType.DMA((FIELDS + 1,)),
        ],
        compiler_params=pltpu.CompilerParams(vmem_limit_bytes=63 << 20),
    )(recovered, combined)


def body(checkpoint, slot_block, live_state, levels, coefficients, tile_owner):
    smem = pl.BlockSpec(memory_space=pltpu.SMEM)
    away = pl.BlockSpec(memory_space=pltpu.HBM)
    dma = pltpu.SemaphoreType.DMA
    recovered, combined = pl.pallas_call(
        kernel,
        name="recover_and_combine",
        out_shape=(
            jax.ShapeDtypeStruct((FIELDS, CZ, CY, CX), jnp.float32),
            jax.ShapeDtypeStruct((4, FIELDS, CZ, 2, CX), jnp.float32),
        ),
        in_specs=[smem, smem, smem, smem, away, away],
        out_specs=(away, pl.BlockSpec(memory_space=pltpu.VMEM)),
        scratch_shapes=[
            *[pltpu.VMEM((64, 4, CX), jnp.float32) for _ in range(FIELDS)],
            pltpu.VMEM((FIELDS, PEERS + 1, CY, CX), jnp.float32),
            pltpu.VMEM((FIELDS, CZ + 2 * HALO, CY, CX), jnp.float32),
            pltpu.VMEM((FIELDS, CZ + 2 * HALO, CY, CX), jnp.float32),
            pltpu.VMEM((FIELDS, CZ + 2 * HALO, CY, CX), jnp.float32),
            pltpu.VMEM((FIELDS, CZ + 2 * HALO, CY, CX), jnp.float32),
            pltpu.VMEM((FIELDS, CZ + 2 * HALO, CY, CX), jnp.float32),
            pltpu.VMEM((FIELDS, CZ + 2 * HALO, CY, CX), jnp.float32),
            pltpu.VMEM((CZ, FIELDS, CY, CX), jnp.float32),
            pltpu.VMEM((FIELDS, CZ, CY, CX), jnp.float32),
            pltpu.VMEM((4, 2, FIELDS, CY, CX), jnp.float32),
            pltpu.VMEM((FIELDS, PEERS, CY, CX), jnp.float32),
            pltpu.VMEM((FIELDS, 17, 2, CX), jnp.float32),
            pltpu.VMEM((FIELDS, PEERS, 4, 2, CX), jnp.float32),
            pltpu.VMEM((16, 128), jnp.int32),
            pltpu.SMEM((16, 128), jnp.int32),
            dma((2 + FIELDS,)),
            dma((FIELDS, PEERS)),
            dma((FIELDS, PEERS)),
            dma((FIELDS, PEERS)),
            dma((FIELDS, PEERS)),
            dma((FIELDS, PEERS)),
            dma((FIELDS, PEERS)),
            dma((FIELDS, PEERS)),
            dma((FIELDS, PEERS)),
            dma((FIELDS, PEERS + 1)),
            dma((FIELDS, 2, HALO)),
            dma((FIELDS, 2)),
            dma((FIELDS, 2)),
            dma((2,)),
            dma((2,)),
        ],
        compiler_params=pltpu.CompilerParams(
            collective_id=0, has_side_effects=True, vmem_limit_bytes=63 << 20
        ),
    )(slot_block, tile_owner, levels, coefficients.reshape(1, 2), checkpoint, live_state)
    return hand_over(recovered[None], combined)


def solution(mesh):
    return jax.shard_map(
        body,
        mesh=mesh,
        in_specs=(
            P("buddy", None, "slab", None, None),
            P(),
            P("buddy", None, "slab", None, None),
            P(None, "buddy", None),
            P(None, "buddy"),
            P("slab", None),
        ),
        out_specs=(P("buddy", None, "slab", None, None), P("buddy", None, "slab", None, None)),
        check_vma=False,
    )
```

```python
import functools

import jax
import jax.numpy as jnp
from jax import lax
from jax.experimental import pallas as pl
from jax.experimental.pallas import tpu as pltpu
from jax.sharding import PartitionSpec as P

MESH = pl.DeviceIdType.MESH
VELOCITY = (0.3, -0.2, 0.45)
FIELDS = 5
CZ = 8
CY = 32
CX = 256
HALO = 4
PEERS = 7
OFFSETS = ((2, 1), (2, 0), (1, 1), (3, 1), (0, 1), (1, 0), (3, 0))


def stencil(levels_ref, kind):
    inverse = []
    for axis in range(3):
        level = levels_ref[kind, 0, axis]
        inverse.append(jnp.where(level == 0, 1.0, jnp.where(level == 1, 2.0, 4.0)).astype(jnp.float32))
    denominator = (abs(VELOCITY[0]) + 1.0) * inverse[0] + (abs(VELOCITY[1]) + 1.0) * inverse[1]
    denominator = denominator + (abs(VELOCITY[2]) + 1.0) * inverse[2]
    step = jnp.max(1.0 / jnp.full((8, 128), denominator, jnp.float32))
    middle = -step * denominator
    sides = []
    for axis in range(3):
        scaled = step * inverse[axis]
        half = 0.5 * (abs(VELOCITY[axis]) + 1.0)
        sides.append(
            (
                scaled * (half - 0.5 * VELOCITY[axis]),
                scaled * (half + 0.5 * VELOCITY[axis]),
                scaled * -0.5,
            )
        )
    return middle, sides


def section(source, base, scalars, share, first, last, write, entry=False):
    middle, sides = scalars
    middle = middle * share
    sides = [tuple(value * share for value in side) for side in sides]
    pairs = [
        (
            (0.5 * (side[0] + side[2]), 0.5 * (side[1] - side[2])),
            (0.5 * (side[0] - side[2]), 0.5 * (side[1] + side[2])),
        )
        for side in sides
    ]
    turns = ((1, CX), (0, CY))

    def turned(axis, q):
        dim, size = turns[axis]
        return (lambda: pltpu.roll(q, size - 1, dim), lambda: pltpu.roll(q, 1, dim))

    def one_layer(z, carry):
        pressure = source[4, z]
        speeds = [source[1 + axis, z] for axis in range(3)]
        pressure_out = base[4, z] + middle * pressure
        results = [None] * FIELDS
        for axis in range(3):
            if axis < 2:
                sums = turned(axis, pressure + speeds[axis])
                gaps = turned(axis, pressure - speeds[axis])
            else:
                up, down = (source[4, z + 1], source[3, z + 1]), (source[4, z - 1], source[3, z - 1])
                sums = (lambda: up[0] + up[1], lambda: down[0] + down[1])
                gaps = (lambda: up[0] - up[1], lambda: down[0] - down[1])
            if VELOCITY[axis] > 0:
                right = pairs[axis][0][1] * sums[1]()
                left = pairs[axis][1][0] * gaps[0]() + pairs[axis][1][1] * gaps[1]()
            else:
                right = pairs[axis][0][0] * sums[0]() + pairs[axis][0][1] * sums[1]()
                left = pairs[axis][1][0] * gaps[0]()
            pressure_out = pressure_out + (right + left)
            out = base[1 + axis, z] + middle * speeds[axis]
            out = out + (right - left)
            for other in range(3):
                if other != axis:
                    if other < 2:
                        plus, minus = (side() for side in turned(other, speeds[axis]))
                    else:
                        plus, minus = source[1 + axis, z + 1], source[1 + axis, z - 1]
                    out = out + (sides[other][0] * plus + sides[other][1] * minus)
            results[1 + axis] = out
        results[4] = pressure_out

        def excess(at):
            return source[0, at] - source[4, at] if entry else source[0, at]

        q = source[0, z] - pressure if entry else source[0, z]
        out = (q if entry else base[0, z] - base[4, z]) + middle * q
        for axis in range(3):
            if axis < 2:
                plus, minus = (side() for side in turned(axis, q))
            else:
                plus, minus = excess(z + 1), excess(z - 1)
            out = out + (sides[axis][0] * plus + sides[axis][1] * minus)
        results[0] = out
        write(z, results)
        return carry

    lax.fori_loop(first, last, one_layer, 0, unroll=2)


def kernel(
    slots_ref,
    owners_ref,
    levels_ref,
    coefficients_ref,
    checkpoint_ref,
    live_ref,
    recovered_ref,
    combined_ref,
    lines_0,
    lines_1,
    lines_2,
    lines_3,
    lines_4,
    packed,
    lost,
    live,
    stage_a,
    stage_b,
    live_a,
    live_b,
    advanced,
    recovered,
    weighted,
    arrived,
    total,
    chosen,
    tables,
    numbers,
    local_sem,
    send1,
    recv1,
    send2,
    recv2,
    send3,
    recv3,
    send4,
    recv4,
    wrap_send,
    wrap_recv,
    halo_send,
    halo_recv,
    live_send,
    live_recv,
):
    lines = (lines_0, lines_1, lines_2, lines_3, lines_4)
    slab = lax.axis_index("slab")
    me = lax.axis_index("buddy")
    slabs = lax.axis_size("slab")
    row, half = me // 2, me % 2
    above = (slab + 1) % slabs
    below = (slab + slabs - 1) % slabs

    def at(offset):
        return ((row + offset[0]) % 4) * 2 + (half + offset[1]) % 2

    peers = [at(offset) for offset in OFFSETS]
    sources = [at(((4 - offset[0]) % 4, offset[1])) for offset in OFFSETS]

    wraps = ((slab % 8 == 0, below, 0, HALO + CZ), (slab % 8 == 7, above, HALO, -HALO))

    barrier = pltpu.get_barrier_semaphore()
    for peer in peers:
        pl.semaphore_signal(barrier, inc=1, device_id={"buddy": peer}, device_id_type=MESH)
    for neighbour in (below, above):
        pl.semaphore_signal(barrier, inc=1, device_id={"slab": neighbour}, device_id_type=MESH)
    for wrap, neighbour, _, _ in wraps:

        @pl.when(wrap)
        def _():
            for peer in peers:
                pl.semaphore_signal(
                    barrier, inc=1, device_id={"slab": neighbour, "buddy": peer}, device_id_type=MESH
                )

    live_in = pltpu.make_async_copy(live_ref.at[0], live.at[:, pl.ds(HALO, CZ)], local_sem.at[0])
    live_in.start()
    own_copies = []
    for field in range(FIELDS):
        copy = pltpu.make_async_copy(
            checkpoint_ref.at[:, field, me], lines[field].at[pl.ds(me * 8, 8)], local_sem.at[1 + field]
        )
        copy.start()
        own_copies.append(copy)

    crossing = jnp.logical_or(wraps[0][0], wraps[1][0])
    pl.semaphore_wait(barrier, jnp.where(crossing, 2 * PEERS + 2, PEERS + 2))

    first_copies = []
    for field in range(FIELDS):
        for i, peer in enumerate(peers):
            copy = pltpu.make_async_remote_copy(
                src_ref=checkpoint_ref.at[:, field, peer],
                dst_ref=lines[field].at[pl.ds(me * 8, 8)],
                send_sem=send1.at[field, i],
                recv_sem=recv1.at[field, i],
                device_id={"buddy": peer},
                device_id_type=MESH,
            )
            copy.start()
            first_copies.append(copy)

    def live_copy(way):
        _, neighbour, first, to = wraps[way]
        return pltpu.make_async_remote_copy(
            src_ref=live_ref.at[0, :, pl.ds(first, HALO)],
            dst_ref=live.at[:, pl.ds(first + to, HALO)],
            send_sem=live_send.at[way],
            recv_sem=live_recv.at[way],
            device_id={"slab": neighbour},
            device_id_type=MESH,
        )

    def start_live(across_the_slice):
        for way in range(2):
            wrap = wraps[way][0]

            @pl.when(wrap if across_the_slice else jnp.logical_not(wrap))
            def _():
                live_copy(way).start()

    start_live(False)

    lanes = lax.broadcasted_iota(jnp.int32, (8, 128), 1)
    held_in = jnp.zeros((8, 128), jnp.int32)
    for slot in range(64):
        held_in = jnp.where(lanes == slots_ref[slot // 8, slot % 8], slot, held_in)
    tables[0:8] = held_in
    owners = [owners_ref[0, tile] for tile in range(16)]
    seated = jnp.full((8, 128), 16, jnp.int32)
    for tile in range(16):
        rank = sum([(owners[before] == owners[tile]).astype(jnp.int32) for before in range(tile)], 0)
        seated = jnp.where(lanes == owners[tile] * 4 + rank, tile, seated)
    tables[8:16] = seated
    tables_in = pltpu.make_async_copy(tables, numbers, local_sem.at[1 + FIELDS])
    tables_in.start()

    tables_in.wait()
    second_copies = []

    def pass_layers(field):
        own_copies[field].wait()
        for i in range(PEERS):
            first_copies[field * PEERS + i].wait_recv()
        for i, peer in enumerate(peers):
            for block in range(8):
                packed[field, i, pl.ds(block * 4, 4), :] = lines[field][numbers[0, peer * 8 + block]]
            copy = pltpu.make_async_remote_copy(
                src_ref=packed.at[field, i],
                dst_ref=lost.at[field, HALO + me],
                send_sem=send2.at[field, i],
                recv_sem=recv2.at[field, i],
                device_id={"buddy": peer},
                device_id_type=MESH,
            )
            copy.start()
            second_copies.append(copy)
        for block in range(8):
            packed[field, PEERS, pl.ds(block * 4, 4), :] = lines[field][numbers[0, me * 8 + block]]
        lost[field, HALO + me] = packed[field, PEERS]
        for i in range(PEERS + 1):
            for way in range(2):
                wrapped(field, i, way, "start")

    def wrapped(field, i, way, action):
        wrap, neighbour, first, to = wraps[way]
        peer = me if i == PEERS else peers[i]
        layer = me - first

        @pl.when(jnp.logical_and(wrap, jnp.logical_and(layer >= 0, layer < HALO)))
        def _():
            copy = pltpu.make_async_remote_copy(
                src_ref=packed.at[field, i],
                dst_ref=lost.at[field, me + to],
                send_sem=wrap_send.at[field, i],
                recv_sem=wrap_recv.at[field, way, layer],
                device_id={"slab": neighbour, "buddy": peer},
                device_id_type=MESH,
            )
            copy.start() if action == "start" else copy.wait_send()

    def to_buffer(buffer):
        def write(z, results):
            for field in range(FIELDS):
                buffer[field, z] = results[field]

        return write

    def to_advanced(z, results):
        results = [results[0] + results[4]] + results[1:]
        for field in range(FIELDS):
            advanced[z - HALO, field] = results[field]

    share = coefficients_ref[0, 0]
    live_share = coefficients_ref[0, 1]

    def to_recovered(z, results):
        results = [results[0] + results[4]] + results[1:]
        for field in range(FIELDS):
            recovered[field, z - HALO] = results[field]
            weighted[(z - HALO) // 2, (z - HALO) % 2, field] = share * results[field] + live_share * advanced[z - HALO, field]

    def to_weighted(z, results):
        results = [results[0] + results[4]] + results[1:]
        for field in range(FIELDS):
            weighted[(z - HALO) // 2, (z - HALO) % 2, field] = (
                share * recovered[field, z - HALO] + live_share * results[field]
            )

    def run_sections(state, scalars, finish):
        section(state, state, scalars, 0.25, 1, 2 * HALO + CZ - 1, to_buffer(stage_a), entry=True)
        section(stage_a, state, scalars, 1.0 / 3.0, 2, 2 * HALO + CZ - 2, to_buffer(stage_b))
        section(stage_b, state, scalars, 0.5, 3, 2 * HALO + CZ - 3, to_buffer(stage_a))
        section(stage_a, state, scalars, 1.0, HALO, HALO + CZ, finish)

    def pass_halos(field):
        for i in range(PEERS):
            second_copies[field * PEERS + i].wait_recv()
        for way in range(2):
            halo(field, way, "start")

    def halo(field, way, action):
        wrap, neighbour, first, to = wraps[way]

        def copy():
            return pltpu.make_async_remote_copy(
                src_ref=lost.at[field, pl.ds(HALO + first, HALO)],
                dst_ref=lost.at[field, pl.ds(first + to, HALO)],
                send_sem=halo_send.at[field, way],
                recv_sem=halo_recv.at[field, way],
                device_id={"slab": neighbour},
                device_id_type=MESH,
            )

        if action == "start" or action == "sent":

            @pl.when(jnp.logical_not(wrap))
            def _():
                copy().start() if action == "start" else copy().wait_send()

        else:
            far = wraps[1 - way][0]

            @pl.when(jnp.logical_not(far))
            def _():
                copy().wait_recv()

            @pl.when(far)
            def _():
                for layer in range(HALO):
                    pltpu.make_async_remote_copy(
                        src_ref=packed.at[field, 0],
                        dst_ref=lost.at[field, first + to + layer],
                        send_sem=wrap_send.at[field, 0],
                        recv_sem=wrap_recv.at[field, way, layer],
                        device_id={"slab": neighbour},
                        device_id_type=MESH,
                    ).wait_recv()

    live_scalars = stencil(levels_ref, 1)
    lost_scalars = stencil(levels_ref, 0)
    last = 2 * HALO + CZ

    def live_section(step, spans, finish):
        source, share_of_step, write = (
            (live, 0.25, to_buffer(live_a)),
            (live_a, 1.0 / 3.0, to_buffer(live_b)),
            (live_b, 0.5, to_buffer(live_a)),
            (live_a, 1.0, finish),
        )[step]
        for first, end in spans:
            section(source, live, live_scalars, share_of_step, first, end, write, entry=step == 0)

    def early_live(step):
        @pl.when(jnp.logical_not(crossing))
        def _():
            if step == 0:
                for way in range(2):
                    live_copy(way).wait_recv()
            live_section(step, ((1 + step, last - 1 - step),), to_advanced)

        if step < 3:

            @pl.when(crossing)
            def _():
                live_section(step, ((HALO + 1 + step, HALO + CZ - 1 - step),), None)

    def late_live():
        @pl.when(crossing)
        def _():
            for way in range(2):
                live_copy(way).wait_recv()
            for step in range(3):
                live_section(
                    step,
                    ((1 + step, HALO + 1 + step), (HALO + CZ - 1 - step, last - 1 - step)),
                    None,
                )
            live_section(3, ((HALO, HALO + CZ),), to_weighted)

    pass_layers(0)
    pass_layers(1)
    pass_layers(2)
    pass_halos(0)
    pass_layers(3)
    pass_halos(1)
    pass_layers(4)
    live_in.wait()
    early_live(0)
    pass_halos(2)
    early_live(1)
    early_live(2)
    pass_halos(3)
    early_live(3)
    start_live(True)
    pass_halos(4)
    for field in range(FIELDS):
        for way in range(2):
            halo(field, way, "received")
    run_sections(lost, lost_scalars, to_recovered)
    late_live()

    recovered_out = pltpu.make_async_copy(recovered, recovered_ref, local_sem.at[0])
    recovered_out.start()

    third_copies = {}
    for field in range(FIELDS):
        for i, peer in enumerate(peers):
            copy = pltpu.make_async_remote_copy(
                src_ref=weighted.at[peer // 2, peer % 2, field],
                dst_ref=arrived.at[field, i],
                send_sem=send3.at[field, i],
                recv_sem=recv3.at[field, i],
                device_id={"buddy": peer},
                device_id_type=MESH,
            )
            copy.start()
            third_copies[field, i] = copy

    for field in range(FIELDS):
        total[field, 16] = jnp.zeros((2, CX), jnp.float32)
    fourth_copies = []
    for field in range(FIELDS):
        summed = weighted[row, half, field]
        for i in range(PEERS):
            third_copies[field, i].wait_recv()
            summed = summed + arrived[field, i]
        for tile in range(16):
            total[field, tile] = summed[2 * tile : 2 * tile + 2]
        for i, peer in enumerate(peers):
            for rank in range(4):
                chosen[field, i, rank] = total[field, numbers[8, peer * 4 + rank]]
            copy = pltpu.make_async_remote_copy(
                src_ref=chosen.at[field, i],
                dst_ref=combined_ref.at[:, field, me],
                send_sem=send4.at[field, i],
                recv_sem=recv4.at[field, i],
                device_id={"buddy": peer},
                device_id_type=MESH,
            )
            copy.start()
            fourth_copies.append(copy)
        for rank in range(4):
            combined_ref[rank, field, me] = total[field, numbers[8, me * 4 + rank]]

    recovered_out.wait()
    for copy in fourth_copies:
        copy.wait()
    for copy in first_copies + second_copies + list(third_copies.values()):
        copy.wait_send()
    for way in range(2):
        live_copy(way).wait_send()
    for field in range(FIELDS):
        for way in range(2):
            halo(field, way, "sent")
            for i in range(PEERS + 1):
                wrapped(field, i, way, "sent")


def hand_over(recovered, combined):
    def copies(recovered_in, combined_in, recovered_out, combined_out, fields, tiles, sem_in, sem_out):
        pairs = [
            (recovered_in.at[0, field], fields.at[field], recovered_out.at[0, field]) for field in range(FIELDS)
        ] + [(combined_in, tiles, combined_out)]
        first = [
            pltpu.make_async_copy(pair[0], pair[1], sem_in.at[i]) for i, pair in enumerate(pairs)
        ]
        second = [
            pltpu.make_async_copy(pair[1], pair[2], sem_out.at[i]) for i, pair in enumerate(pairs)
        ]
        for copy in first:
            copy.start()
        for before, after in zip(first, second):
            before.wait()
            after.start()
        for copy in second:
            copy.wait()

    away = pl.BlockSpec(memory_space=pltpu.HBM)
    return pl.pallas_call(
        copies,
        name="hand_over",
        out_shape=(
            jax.ShapeDtypeStruct(recovered.shape, recovered.dtype),
            jax.ShapeDtypeStruct(combined.shape, combined.dtype),
        ),
        in_specs=[away, away],
        out_specs=(away, away),
        scratch_shapes=[
            pltpu.VMEM(recovered.shape[1:], jnp.float32),
            pltpu.VMEM(combined.shape, jnp.float32),
            pltpu.SemaphoreType.DMA((FIELDS + 1,)),
            pltpu.SemaphoreType.DMA((FIELDS + 1,)),
        ],
        compiler_params=pltpu.CompilerParams(vmem_limit_bytes=63 << 20),
    )(recovered, combined)


def body(checkpoint, slot_block, live_state, levels, coefficients, tile_owner):
    smem = pl.BlockSpec(memory_space=pltpu.SMEM)
    away = pl.BlockSpec(memory_space=pltpu.HBM)
    dma = pltpu.SemaphoreType.DMA
    recovered, combined = pl.pallas_call(
        kernel,
        name="recover_and_combine",
        out_shape=(
            jax.ShapeDtypeStruct((FIELDS, CZ, CY, CX), jnp.float32),
            jax.ShapeDtypeStruct((4, FIELDS, CZ, 2, CX), jnp.float32),
        ),
        in_specs=[smem, smem, smem, smem, away, away],
        out_specs=(away, pl.BlockSpec(memory_space=pltpu.VMEM)),
        scratch_shapes=[
            *[pltpu.VMEM((64, 4, CX), jnp.float32) for _ in range(FIELDS)],
            pltpu.VMEM((FIELDS, PEERS + 1, CY, CX), jnp.float32),
            pltpu.VMEM((FIELDS, CZ + 2 * HALO, CY, CX), jnp.float32),
            pltpu.VMEM((FIELDS, CZ + 2 * HALO, CY, CX), jnp.float32),
            pltpu.VMEM((FIELDS, CZ + 2 * HALO, CY, CX), jnp.float32),
            pltpu.VMEM((FIELDS, CZ + 2 * HALO, CY, CX), jnp.float32),
            pltpu.VMEM((FIELDS, CZ + 2 * HALO, CY, CX), jnp.float32),
            pltpu.VMEM((FIELDS, CZ + 2 * HALO, CY, CX), jnp.float32),
            pltpu.VMEM((CZ, FIELDS, CY, CX), jnp.float32),
            pltpu.VMEM((FIELDS, CZ, CY, CX), jnp.float32),
            pltpu.VMEM((4, 2, FIELDS, CY, CX), jnp.float32),
            pltpu.VMEM((FIELDS, PEERS, CY, CX), jnp.float32),
            pltpu.VMEM((FIELDS, 17, 2, CX), jnp.float32),
            pltpu.VMEM((FIELDS, PEERS, 4, 2, CX), jnp.float32),
            pltpu.VMEM((16, 128), jnp.int32),
            pltpu.SMEM((16, 128), jnp.int32),
            dma((2 + FIELDS,)),
            dma((FIELDS, PEERS)),
            dma((FIELDS, PEERS)),
            dma((FIELDS, PEERS)),
            dma((FIELDS, PEERS)),
            dma((FIELDS, PEERS)),
            dma((FIELDS, PEERS)),
            dma((FIELDS, PEERS)),
            dma((FIELDS, PEERS)),
            dma((FIELDS, PEERS + 1)),
            dma((FIELDS, 2, HALO)),
            dma((FIELDS, 2)),
            dma((FIELDS, 2)),
            dma((2,)),
            dma((2,)),
        ],
        compiler_params=pltpu.CompilerParams(
            collective_id=0, has_side_effects=True, vmem_limit_bytes=63 << 20
        ),
    )(slot_block, tile_owner, levels, coefficients.reshape(1, 2), checkpoint, live_state)
    return hand_over(recovered[None], combined)


def solution(mesh):
    return jax.shard_map(
        body,
        mesh=mesh,
        in_specs=(
            P("buddy", None, "slab", None, None),
            P(),
            P("buddy", None, "slab", None, None),
            P(None, "buddy", None),
            P(None, "buddy"),
            P("slab", None),
        ),
        out_specs=(P("buddy", None, "slab", None, None), P("buddy", None, "slab", None, None)),
        check_vma=False,
    )
```

```python
import functools

import jax
import jax.numpy as jnp
from jax import lax
from jax.experimental import pallas as pl
from jax.experimental.pallas import tpu as pltpu
from jax.sharding import PartitionSpec as P

MESH = pl.DeviceIdType.MESH
VELOCITY = (0.3, -0.2, 0.45)
FIELDS = 5
CZ = 8
CY = 32
CX = 256
HALO = 4
PEERS = 7
OFFSETS = ((2, 1), (1, 1), (3, 1), (0, 1), (2, 0), (1, 0), (3, 0))


def stencil(levels_ref, kind):
    inverse = []
    for axis in range(3):
        level = levels_ref[kind, 0, axis]
        inverse.append(jnp.where(level == 0, 1.0, jnp.where(level == 1, 2.0, 4.0)).astype(jnp.float32))
    denominator = (abs(VELOCITY[0]) + 1.0) * inverse[0] + (abs(VELOCITY[1]) + 1.0) * inverse[1]
    denominator = denominator + (abs(VELOCITY[2]) + 1.0) * inverse[2]
    step = jnp.max(1.0 / jnp.full((8, 128), denominator, jnp.float32))
    middle = -step * denominator
    sides = []
    for axis in range(3):
        scaled = step * inverse[axis]
        half = 0.5 * (abs(VELOCITY[axis]) + 1.0)
        sides.append(
            (
                scaled * (half - 0.5 * VELOCITY[axis]),
                scaled * (half + 0.5 * VELOCITY[axis]),
                scaled * -0.5,
            )
        )
    return middle, sides


def section(source, base, scalars, share, first, count, write, entry=False):
    middle, sides = scalars
    middle = middle * share
    sides = [tuple(value * share for value in side) for side in sides]
    pairs = [
        (
            (0.5 * (side[0] + side[2]), 0.5 * (side[1] - side[2])),
            (0.5 * (side[0] - side[2]), 0.5 * (side[1] + side[2])),
        )
        for side in sides
    ]
    turns = ((1, CX), (0, CY))

    def turned(axis, q):
        dim, size = turns[axis]
        return (lambda: pltpu.roll(q, size - 1, dim), lambda: pltpu.roll(q, 1, dim))

    def one_layer(i, carry):
        z = first + i
        pressure = source[4, z]
        speeds = [source[1 + axis, z] for axis in range(3)]
        pressure_out = base[4, z] + middle * pressure
        results = [None] * FIELDS
        for axis in range(3):
            if axis < 2:
                sums = turned(axis, pressure + speeds[axis])
                gaps = turned(axis, pressure - speeds[axis])
            else:
                up, down = (source[4, z + 1], source[3, z + 1]), (source[4, z - 1], source[3, z - 1])
                sums = (lambda: up[0] + up[1], lambda: down[0] + down[1])
                gaps = (lambda: up[0] - up[1], lambda: down[0] - down[1])
            if VELOCITY[axis] > 0:
                right = pairs[axis][0][1] * sums[1]()
                left = pairs[axis][1][0] * gaps[0]() + pairs[axis][1][1] * gaps[1]()
            else:
                right = pairs[axis][0][0] * sums[0]() + pairs[axis][0][1] * sums[1]()
                left = pairs[axis][1][0] * gaps[0]()
            pressure_out = pressure_out + (right + left)
            out = base[1 + axis, z] + middle * speeds[axis]
            out = out + (right - left)
            for other in range(3):
                if other != axis:
                    if other < 2:
                        plus, minus = (side() for side in turned(other, speeds[axis]))
                    else:
                        plus, minus = source[1 + axis, z + 1], source[1 + axis, z - 1]
                    out = out + (sides[other][0] * plus + sides[other][1] * minus)
            results[1 + axis] = out
        results[4] = pressure_out

        def excess(at):
            return source[0, at] - source[4, at] if entry else source[0, at]

        q = source[0, z] - pressure if entry else source[0, z]
        out = (q if entry else base[0, z] - base[4, z]) + middle * q
        for axis in range(3):
            if axis < 2:
                plus, minus = (side() for side in turned(axis, q))
            else:
                plus, minus = excess(z + 1), excess(z - 1)
            out = out + (sides[axis][0] * plus + sides[axis][1] * minus)
        results[0] = out
        write(z, results)
        return carry

    lax.fori_loop(0, count, one_layer, 0, unroll=2)


def kernel(
    slots_ref,
    owners_ref,
    levels_ref,
    coefficients_ref,
    checkpoint_ref,
    live_ref,
    recovered_ref,
    combined_ref,
    lines_0,
    lines_1,
    lines_2,
    lines_3,
    lines_4,
    packed,
    lost,
    live,
    stage_a,
    stage_b,
    live_a,
    live_b,
    advanced,
    recovered,
    weighted,
    arrived,
    total,
    chosen,
    tables,
    numbers,
    local_sem,
    send1,
    recv1,
    send2,
    recv2,
    send3,
    recv3,
    send4,
    recv4,
    wrap_send,
    wrap_recv,
    halo_send,
    halo_recv,
    live_send,
    live_recv,
):
    lines = (lines_0, lines_1, lines_2, lines_3, lines_4)
    slab = lax.axis_index("slab")
    me = lax.axis_index("buddy")
    slabs = lax.axis_size("slab")
    row, half = me // 2, me % 2
    above = (slab + 1) % slabs
    below = (slab + slabs - 1) % slabs

    def at(offset):
        return ((row + offset[0]) % 4) * 2 + (half + offset[1]) % 2

    peers = [at(offset) for offset in OFFSETS]
    sources = [at(((4 - offset[0]) % 4, offset[1])) for offset in OFFSETS]

    wraps = ((slab % 8 == 0, below, 0, HALO + CZ), (slab % 8 == 7, above, HALO, -HALO))

    barrier = pltpu.get_barrier_semaphore()
    for peer in peers:
        pl.semaphore_signal(barrier, inc=1, device_id={"buddy": peer}, device_id_type=MESH)
    for neighbour in (below, above):
        pl.semaphore_signal(barrier, inc=1, device_id={"slab": neighbour}, device_id_type=MESH)
    for wrap, neighbour, _, _ in wraps:

        @pl.when(wrap)
        def _():
            for peer in peers:
                pl.semaphore_signal(
                    barrier, inc=1, device_id={"slab": neighbour, "buddy": peer}, device_id_type=MESH
                )

    live_in = pltpu.make_async_copy(live_ref.at[0], live.at[:, pl.ds(HALO, CZ)], local_sem.at[0])
    live_in.start()
    own_copies = []
    for field in range(FIELDS):
        copy = pltpu.make_async_copy(
            checkpoint_ref.at[:, field, me], lines[field].at[pl.ds(me * 8, 8)], local_sem.at[1 + field]
        )
        copy.start()
        own_copies.append(copy)

    crossing = jnp.logical_or(wraps[0][0], wraps[1][0])
    pl.semaphore_wait(barrier, jnp.where(crossing, 2 * PEERS + 2, PEERS + 2))

    first_copies = []
    for field in range(FIELDS):
        for i, peer in enumerate(peers):
            copy = pltpu.make_async_remote_copy(
                src_ref=checkpoint_ref.at[:, field, peer],
                dst_ref=lines[field].at[pl.ds(me * 8, 8)],
                send_sem=send1.at[field, i],
                recv_sem=recv1.at[field, i],
                device_id={"buddy": peer},
                device_id_type=MESH,
            )
            copy.start()
            first_copies.append(copy)

    def live_copy(way):
        _, neighbour, first, to = wraps[way]
        return pltpu.make_async_remote_copy(
            src_ref=live_ref.at[0, :, pl.ds(first, HALO)],
            dst_ref=live.at[:, pl.ds(first + to, HALO)],
            send_sem=live_send.at[way],
            recv_sem=live_recv.at[way],
            device_id={"slab": neighbour},
            device_id_type=MESH,
        )

    def start_live(across_the_slice):
        for way in range(2):
            wrap = wraps[way][0]

            @pl.when(wrap if across_the_slice else jnp.logical_not(wrap))
            def _():
                live_copy(way).start()

    start_live(False)

    lanes = lax.broadcasted_iota(jnp.int32, (8, 128), 1)
    held_in = jnp.zeros((8, 128), jnp.int32)
    for slot in range(64):
        held_in = jnp.where(lanes == slots_ref[slot // 8, slot % 8], slot, held_in)
    tables[0:8] = held_in
    owners = [owners_ref[0, tile] for tile in range(16)]
    seated = jnp.full((8, 128), 16, jnp.int32)
    for tile in range(16):
        rank = sum([(owners[before] == owners[tile]).astype(jnp.int32) for before in range(tile)], 0)
        seated = jnp.where(lanes == owners[tile] * 4 + rank, tile, seated)
    tables[8:16] = seated
    tables_in = pltpu.make_async_copy(tables, numbers, local_sem.at[1 + FIELDS])
    tables_in.start()

    tables_in.wait()
    second_copies = []

    def pass_layers(field):
        own_copies[field].wait()
        for i in range(PEERS):
            first_copies[field * PEERS + i].wait_recv()
        for i, peer in enumerate(peers):
            for block in range(8):
                packed[field, i, pl.ds(block * 4, 4), :] = lines[field][numbers[0, peer * 8 + block]]
            copy = pltpu.make_async_remote_copy(
                src_ref=packed.at[field, i],
                dst_ref=lost.at[field, HALO + me],
                send_sem=send2.at[field, i],
                recv_sem=recv2.at[field, i],
                device_id={"buddy": peer},
                device_id_type=MESH,
            )
            copy.start()
            second_copies.append(copy)
        for block in range(8):
            packed[field, PEERS, pl.ds(block * 4, 4), :] = lines[field][numbers[0, me * 8 + block]]
        lost[field, HALO + me] = packed[field, PEERS]
        for i in range(PEERS + 1):
            for way in range(2):
                wrapped(field, i, way, "start")

    def wrapped(field, i, way, action):
        wrap, neighbour, first, to = wraps[way]
        peer = me if i == PEERS else peers[i]
        layer = me - first

        @pl.when(jnp.logical_and(wrap, jnp.logical_and(layer >= 0, layer < HALO)))
        def _():
            copy = pltpu.make_async_remote_copy(
                src_ref=packed.at[field, i],
                dst_ref=lost.at[field, me + to],
                send_sem=wrap_send.at[field, i],
                recv_sem=wrap_recv.at[field, way, layer],
                device_id={"slab": neighbour, "buddy": peer},
                device_id_type=MESH,
            )
            copy.start() if action == "start" else copy.wait_send()

    def to_buffer(buffer):
        def write(z, results):
            for field in range(FIELDS):
                buffer[field, z] = results[field]

        return write

    def to_advanced(z, results):
        results = [results[0] + results[4]] + results[1:]
        for field in range(FIELDS):
            advanced[z - HALO, field] = results[field]

    share = coefficients_ref[0, 0]
    live_share = coefficients_ref[0, 1]

    def to_recovered(z, results):
        results = [results[0] + results[4]] + results[1:]
        for field in range(FIELDS):
            recovered[field, z - HALO] = results[field]
            weighted[(z - HALO) // 2, (z - HALO) % 2, field] = share * results[field] + live_share * advanced[z - HALO, field]

    def to_weighted(z, results):
        results = [results[0] + results[4]] + results[1:]
        for field in range(FIELDS):
            weighted[(z - HALO) // 2, (z - HALO) % 2, field] = (
                share * recovered[field, z - HALO] + live_share * results[field]
            )

    def run_sections(state, scalars, finish):
        section(state, state, scalars, 0.25, 1, 2 * HALO + CZ - 2, to_buffer(stage_a), entry=True)
        section(stage_a, state, scalars, 1.0 / 3.0, 2, 2 * HALO + CZ - 4, to_buffer(stage_b))
        section(stage_b, state, scalars, 0.5, 3, 2 * HALO + CZ - 6, to_buffer(stage_a))
        section(stage_a, state, scalars, 1.0, HALO, CZ, finish)

    def pass_halos(field):
        for i in range(PEERS):
            second_copies[field * PEERS + i].wait_recv()
        for way in range(2):
            halo(field, way, "start")

    def halo(field, way, action):
        wrap, neighbour, first, to = wraps[way]

        def copy():
            return pltpu.make_async_remote_copy(
                src_ref=lost.at[field, pl.ds(HALO + first, HALO)],
                dst_ref=lost.at[field, pl.ds(first + to, HALO)],
                send_sem=halo_send.at[field, way],
                recv_sem=halo_recv.at[field, way],
                device_id={"slab": neighbour},
                device_id_type=MESH,
            )

        if action == "start" or action == "sent":

            @pl.when(jnp.logical_not(wrap))
            def _():
                copy().start() if action == "start" else copy().wait_send()

        else:
            far = wraps[1 - way][0]

            @pl.when(jnp.logical_not(far))
            def _():
                copy().wait_recv()

            @pl.when(far)
            def _():
                for layer in range(HALO):
                    pltpu.make_async_remote_copy(
                        src_ref=packed.at[field, 0],
                        dst_ref=lost.at[field, first + to + layer],
                        send_sem=wrap_send.at[field, 0],
                        recv_sem=wrap_recv.at[field, way, layer],
                        device_id={"slab": neighbour},
                        device_id_type=MESH,
                    ).wait_recv()

    live_scalars = stencil(levels_ref, 1)
    lost_scalars = stencil(levels_ref, 0)

    def live_section(step, first, count, finish):
        source, share_of_step, write = (
            (live, 0.25, to_buffer(live_a)),
            (live_a, 1.0 / 3.0, to_buffer(live_b)),
            (live_b, 0.5, to_buffer(live_a)),
            (live_a, 1.0, finish),
        )[step]
        section(source, live, live_scalars, share_of_step, first, count, write, entry=step == 0)

    late_below = slab % 8 == 0

    def live_received(late):
        for way in range(2):
            far = wraps[1 - way][0]

            @pl.when(far if late else jnp.logical_not(far))
            def _():
                live_copy(way).wait_recv()

    def early_live(step):
        if step == 0:
            live_received(False)

        @pl.when(jnp.logical_not(crossing))
        def _():
            live_section(step, 1 + step, 2 * HALO + CZ - 2 - 2 * step, to_advanced)

        @pl.when(crossing)
        def _():
            first = jnp.where(late_below, HALO + 1 + step, 1 + step)
            live_section(step, first, HALO + CZ - 2 - 2 * step, to_advanced)

    def late_live():
        live_received(True)

        @pl.when(crossing)
        def _():
            for step in range(4):
                first = jnp.where(late_below, 1 + step, HALO + CZ - 1 - step)
                live_section(step, first, HALO, to_weighted)

    pass_layers(0)
    pass_layers(1)
    pass_layers(2)
    pass_halos(0)
    pass_layers(3)
    pass_halos(1)
    pass_layers(4)
    live_in.wait()
    early_live(0)
    pass_halos(2)
    early_live(1)
    early_live(2)
    pass_halos(3)
    early_live(3)
    start_live(True)
    pass_halos(4)
    for field in range(FIELDS):
        for way in range(2):
            halo(field, way, "received")
    run_sections(lost, lost_scalars, to_recovered)

    third_copies = {}
    for field in range(FIELDS):
        for i, peer in enumerate(peers):
            third_copies[field, i] = pltpu.make_async_remote_copy(
                src_ref=weighted.at[peer // 2, peer % 2, field],
                dst_ref=arrived.at[field, i],
                send_sem=send3.at[field, i],
                recv_sem=recv3.at[field, i],
                device_id={"buddy": peer},
                device_id_type=MESH,
            )

    def send_layers(late):
        for field in range(FIELDS):
            for i, peer in enumerate(peers):
                is_late = jnp.logical_and(crossing, (peer < HALO) == late_below)

                @pl.when(is_late if late else jnp.logical_not(is_late))
                def _():
                    third_copies[field, i].start()

    send_layers(False)
    late_live()
    send_layers(True)

    recovered_out = pltpu.make_async_copy(recovered, recovered_ref, local_sem.at[0])
    recovered_out.start()

    for field in range(FIELDS):
        total[field, 16] = jnp.zeros((2, CX), jnp.float32)
    fourth_copies = []
    for field in range(FIELDS):
        summed = weighted[row, half, field]
        for i in range(PEERS):
            third_copies[field, i].wait_recv()
            summed = summed + arrived[field, i]
        for tile in range(16):
            total[field, tile] = summed[2 * tile : 2 * tile + 2]
        for i, peer in enumerate(peers):
            for rank in range(4):
                chosen[field, i, rank] = total[field, numbers[8, peer * 4 + rank]]
            copy = pltpu.make_async_remote_copy(
                src_ref=chosen.at[field, i],
                dst_ref=combined_ref.at[:, field, me],
                send_sem=send4.at[field, i],
                recv_sem=recv4.at[field, i],
                device_id={"buddy": peer},
                device_id_type=MESH,
            )
            copy.start()
            fourth_copies.append(copy)
        for rank in range(4):
            combined_ref[rank, field, me] = total[field, numbers[8, me * 4 + rank]]

    recovered_out.wait()
    for copy in fourth_copies:
        copy.wait()
    for copy in first_copies + second_copies + list(third_copies.values()):
        copy.wait_send()
    for way in range(2):
        live_copy(way).wait_send()
    for field in range(FIELDS):
        for way in range(2):
            halo(field, way, "sent")
            for i in range(PEERS + 1):
                wrapped(field, i, way, "sent")


def hand_over(recovered, combined):
    def copies(recovered_in, combined_in, recovered_out, combined_out, fields, tiles, sem_in, sem_out):
        pairs = [
            (recovered_in.at[0, field], fields.at[field], recovered_out.at[0, field]) for field in range(FIELDS)
        ] + [(combined_in, tiles, combined_out)]
        first = [
            pltpu.make_async_copy(pair[0], pair[1], sem_in.at[i]) for i, pair in enumerate(pairs)
        ]
        second = [
            pltpu.make_async_copy(pair[1], pair[2], sem_out.at[i]) for i, pair in enumerate(pairs)
        ]
        for copy in first:
            copy.start()
        for before, after in zip(first, second):
            before.wait()
            after.start()
        for copy in second:
            copy.wait()

    away = pl.BlockSpec(memory_space=pltpu.HBM)
    return pl.pallas_call(
        copies,
        name="hand_over",
        out_shape=(
            jax.ShapeDtypeStruct(recovered.shape, recovered.dtype),
            jax.ShapeDtypeStruct(combined.shape, combined.dtype),
        ),
        in_specs=[away, away],
        out_specs=(away, away),
        scratch_shapes=[
            pltpu.VMEM(recovered.shape[1:], jnp.float32),
            pltpu.VMEM(combined.shape, jnp.float32),
            pltpu.SemaphoreType.DMA((FIELDS + 1,)),
            pltpu.SemaphoreType.DMA((FIELDS + 1,)),
        ],
        compiler_params=pltpu.CompilerParams(vmem_limit_bytes=63 << 20),
    )(recovered, combined)


def body(checkpoint, slot_block, live_state, levels, coefficients, tile_owner):
    smem = pl.BlockSpec(memory_space=pltpu.SMEM)
    away = pl.BlockSpec(memory_space=pltpu.HBM)
    dma = pltpu.SemaphoreType.DMA
    recovered, combined = pl.pallas_call(
        kernel,
        name="recover_and_combine",
        out_shape=(
            jax.ShapeDtypeStruct((FIELDS, CZ, CY, CX), jnp.float32),
            jax.ShapeDtypeStruct((4, FIELDS, CZ, 2, CX), jnp.float32),
        ),
        in_specs=[smem, smem, smem, smem, away, away],
        out_specs=(away, pl.BlockSpec(memory_space=pltpu.VMEM)),
        scratch_shapes=[
            *[pltpu.VMEM((64, 4, CX), jnp.float32) for _ in range(FIELDS)],
            pltpu.VMEM((FIELDS, PEERS + 1, CY, CX), jnp.float32),
            pltpu.VMEM((FIELDS, CZ + 2 * HALO, CY, CX), jnp.float32),
            pltpu.VMEM((FIELDS, CZ + 2 * HALO, CY, CX), jnp.float32),
            pltpu.VMEM((FIELDS, CZ + 2 * HALO, CY, CX), jnp.float32),
            pltpu.VMEM((FIELDS, CZ + 2 * HALO, CY, CX), jnp.float32),
            pltpu.VMEM((FIELDS, CZ + 2 * HALO, CY, CX), jnp.float32),
            pltpu.VMEM((FIELDS, CZ + 2 * HALO, CY, CX), jnp.float32),
            pltpu.VMEM((CZ, FIELDS, CY, CX), jnp.float32),
            pltpu.VMEM((FIELDS, CZ, CY, CX), jnp.float32),
            pltpu.VMEM((4, 2, FIELDS, CY, CX), jnp.float32),
            pltpu.VMEM((FIELDS, PEERS, CY, CX), jnp.float32),
            pltpu.VMEM((FIELDS, 17, 2, CX), jnp.float32),
            pltpu.VMEM((FIELDS, PEERS, 4, 2, CX), jnp.float32),
            pltpu.VMEM((16, 128), jnp.int32),
            pltpu.SMEM((16, 128), jnp.int32),
            dma((2 + FIELDS,)),
            dma((FIELDS, PEERS)),
            dma((FIELDS, PEERS)),
            dma((FIELDS, PEERS)),
            dma((FIELDS, PEERS)),
            dma((FIELDS, PEERS)),
            dma((FIELDS, PEERS)),
            dma((FIELDS, PEERS)),
            dma((FIELDS, PEERS)),
            dma((FIELDS, PEERS + 1)),
            dma((FIELDS, 2, HALO)),
            dma((FIELDS, 2)),
            dma((FIELDS, 2)),
            dma((2,)),
            dma((2,)),
        ],
        compiler_params=pltpu.CompilerParams(
            collective_id=0, has_side_effects=True, vmem_limit_bytes=63 << 20
        ),
    )(slot_block, tile_owner, levels, coefficients.reshape(1, 2), checkpoint, live_state)
    return hand_over(recovered[None], combined)


def solution(mesh):
    return jax.shard_map(
        body,
        mesh=mesh,
        in_specs=(
            P("buddy", None, "slab", None, None),
            P(),
            P("buddy", None, "slab", None, None),
            P(None, "buddy", None),
            P(None, "buddy"),
            P("slab", None),
        ),
        out_specs=(P("buddy", None, "slab", None, None), P("buddy", None, "slab", None, None)),
        check_vma=False,
    )
```

```python
import functools

import jax
import jax.numpy as jnp
from jax import lax
from jax.experimental import pallas as pl
from jax.experimental.pallas import tpu as pltpu
from jax.sharding import PartitionSpec as P

MESH = pl.DeviceIdType.MESH
VELOCITY = (0.3, -0.2, 0.45)
FIELDS = 5
CZ = 8
CY = 32
CX = 256
HALO = 4
PEERS = 7
OFFSETS = ((0, 1), (2, 1), (1, 1), (3, 1), (2, 0), (1, 0), (3, 0))


def stencil(levels_ref, kind):
    inverse = []
    for axis in range(3):
        level = levels_ref[kind, 0, axis]
        inverse.append(jnp.where(level == 0, 1.0, jnp.where(level == 1, 2.0, 4.0)).astype(jnp.float32))
    denominator = (abs(VELOCITY[0]) + 1.0) * inverse[0] + (abs(VELOCITY[1]) + 1.0) * inverse[1]
    denominator = denominator + (abs(VELOCITY[2]) + 1.0) * inverse[2]
    step = jnp.max(1.0 / jnp.full((8, 128), denominator, jnp.float32))
    middle = -step * denominator
    sides = []
    for axis in range(3):
        scaled = step * inverse[axis]
        half = 0.5 * (abs(VELOCITY[axis]) + 1.0)
        sides.append(
            (
                scaled * (half - 0.5 * VELOCITY[axis]),
                scaled * (half + 0.5 * VELOCITY[axis]),
                scaled * -0.5,
            )
        )
    return middle, sides


def section(source, base, scalars, share, first, count, write, entry=False):
    middle, sides = scalars
    middle = middle * share
    sides = [tuple(value * share for value in side) for side in sides]
    pairs = [
        (
            (0.5 * (side[0] + side[2]), 0.5 * (side[1] - side[2])),
            (0.5 * (side[0] - side[2]), 0.5 * (side[1] + side[2])),
        )
        for side in sides
    ]
    turns = ((1, CX), (0, CY))

    def turned(axis, q):
        dim, size = turns[axis]
        return (lambda: pltpu.roll(q, size - 1, dim), lambda: pltpu.roll(q, 1, dim))

    def one_layer(i, carry):
        z = first + i
        pressure = source[4, z]
        speeds = [source[1 + axis, z] for axis in range(3)]
        pressure_out = base[4, z] + middle * pressure
        results = [None] * FIELDS
        for axis in range(3):
            if axis < 2:
                sums = turned(axis, pressure + speeds[axis])
                gaps = turned(axis, pressure - speeds[axis])
            else:
                up, down = (source[4, z + 1], source[3, z + 1]), (source[4, z - 1], source[3, z - 1])
                sums = (lambda: up[0] + up[1], lambda: down[0] + down[1])
                gaps = (lambda: up[0] - up[1], lambda: down[0] - down[1])
            if VELOCITY[axis] > 0:
                right = pairs[axis][0][1] * sums[1]()
                left = pairs[axis][1][0] * gaps[0]() + pairs[axis][1][1] * gaps[1]()
            else:
                right = pairs[axis][0][0] * sums[0]() + pairs[axis][0][1] * sums[1]()
                left = pairs[axis][1][0] * gaps[0]()
            pressure_out = pressure_out + (right + left)
            out = base[1 + axis, z] + middle * speeds[axis]
            out = out + (right - left)
            for other in range(3):
                if other != axis:
                    if other < 2:
                        plus, minus = (side() for side in turned(other, speeds[axis]))
                    else:
                        plus, minus = source[1 + axis, z + 1], source[1 + axis, z - 1]
                    out = out + (sides[other][0] * plus + sides[other][1] * minus)
            results[1 + axis] = out
        results[4] = pressure_out

        def excess(at):
            return source[0, at] - source[4, at] if entry else source[0, at]

        q = source[0, z] - pressure if entry else source[0, z]
        out = (q if entry else base[0, z] - base[4, z]) + middle * q
        for axis in range(3):
            if axis < 2:
                plus, minus = (side() for side in turned(axis, q))
            else:
                plus, minus = excess(z + 1), excess(z - 1)
            out = out + (sides[axis][0] * plus + sides[axis][1] * minus)
        results[0] = out
        write(z, results)
        return carry

    lax.fori_loop(0, count, one_layer, 0, unroll=2)


def kernel(
    slots_ref,
    owners_ref,
    levels_ref,
    coefficients_ref,
    checkpoint_ref,
    live_ref,
    recovered_ref,
    combined_ref,
    lines_0,
    lines_1,
    lines_2,
    lines_3,
    lines_4,
    packed,
    lost,
    live,
    stage_a,
    stage_b,
    live_a,
    live_b,
    advanced,
    recovered,
    weighted,
    arrived,
    total,
    chosen,
    tables,
    numbers,
    local_sem,
    send1,
    recv1,
    send2,
    recv2,
    send3,
    recv3,
    send4,
    recv4,
    wrap_send,
    wrap_recv,
    halo_send,
    halo_recv,
    live_send,
    live_recv,
):
    lines = (lines_0, lines_1, lines_2, lines_3, lines_4)
    slab = lax.axis_index("slab")
    me = lax.axis_index("buddy")
    slabs = lax.axis_size("slab")
    row, half = me // 2, me % 2
    above = (slab + 1) % slabs
    below = (slab + slabs - 1) % slabs

    def at(offset):
        return ((row + offset[0]) % 4) * 2 + (half + offset[1]) % 2

    peers = [at(offset) for offset in OFFSETS]
    sources = [at(((4 - offset[0]) % 4, offset[1])) for offset in OFFSETS]

    wraps = ((slab % 8 == 0, below, 0, HALO + CZ), (slab % 8 == 7, above, HALO, -HALO))

    barrier = pltpu.get_barrier_semaphore()
    for peer in peers:
        pl.semaphore_signal(barrier, inc=1, device_id={"buddy": peer}, device_id_type=MESH)
    for neighbour in (below, above):
        pl.semaphore_signal(barrier, inc=1, device_id={"slab": neighbour}, device_id_type=MESH)
    for wrap, neighbour, _, _ in wraps:

        @pl.when(wrap)
        def _():
            for peer in peers:
                pl.semaphore_signal(
                    barrier, inc=1, device_id={"slab": neighbour, "buddy": peer}, device_id_type=MESH
                )

    live_in = pltpu.make_async_copy(live_ref.at[0], live.at[:, pl.ds(HALO, CZ)], local_sem.at[0])
    live_in.start()
    own_copies = []
    for field in range(FIELDS):
        copy = pltpu.make_async_copy(
            checkpoint_ref.at[:, field, me], lines[field].at[pl.ds(me * 8, 8)], local_sem.at[1 + field]
        )
        copy.start()
        own_copies.append(copy)

    crossing = jnp.logical_or(wraps[0][0], wraps[1][0])
    pl.semaphore_wait(barrier, jnp.where(crossing, 2 * PEERS + 2, PEERS + 2))

    first_copies = []
    for field in range(FIELDS):
        for i, peer in enumerate(peers):
            copy = pltpu.make_async_remote_copy(
                src_ref=checkpoint_ref.at[:, field, peer],
                dst_ref=lines[field].at[pl.ds(me * 8, 8)],
                send_sem=send1.at[field, i],
                recv_sem=recv1.at[field, i],
                device_id={"buddy": peer},
                device_id_type=MESH,
            )
            copy.start()
            first_copies.append(copy)

    def live_copy(way):
        _, neighbour, first, to = wraps[way]
        return pltpu.make_async_remote_copy(
            src_ref=live_ref.at[0, :, pl.ds(first, HALO)],
            dst_ref=live.at[:, pl.ds(first + to, HALO)],
            send_sem=live_send.at[way],
            recv_sem=live_recv.at[way],
            device_id={"slab": neighbour},
            device_id_type=MESH,
        )

    def start_live(across_the_slice):
        for way in range(2):
            wrap = wraps[way][0]

            @pl.when(wrap if across_the_slice else jnp.logical_not(wrap))
            def _():
                live_copy(way).start()

    start_live(False)

    lanes = lax.broadcasted_iota(jnp.int32, (8, 128), 1)
    held_in = jnp.zeros((8, 128), jnp.int32)
    for slot in range(64):
        held_in = jnp.where(lanes == slots_ref[slot // 8, slot % 8], slot, held_in)
    tables[0:8] = held_in
    owners = [owners_ref[0, tile] for tile in range(16)]
    seated = jnp.full((8, 128), 16, jnp.int32)
    for tile in range(16):
        rank = sum([(owners[before] == owners[tile]).astype(jnp.int32) for before in range(tile)], 0)
        seated = jnp.where(lanes == owners[tile] * 4 + rank, tile, seated)
    tables[8:16] = seated
    tables_in = pltpu.make_async_copy(tables, numbers, local_sem.at[1 + FIELDS])
    tables_in.start()

    tables_in.wait()
    second_copies = []

    def pass_layers(field):
        own_copies[field].wait()
        for i in range(PEERS):
            first_copies[field * PEERS + i].wait_recv()
        for i, peer in enumerate(peers):
            for block in range(8):
                packed[field, i, pl.ds(block * 4, 4), :] = lines[field][numbers[0, peer * 8 + block]]
            copy = pltpu.make_async_remote_copy(
                src_ref=packed.at[field, i],
                dst_ref=lost.at[field, HALO + me],
                send_sem=send2.at[field, i],
                recv_sem=recv2.at[field, i],
                device_id={"buddy": peer},
                device_id_type=MESH,
            )
            copy.start()
            second_copies.append(copy)
        for block in range(8):
            packed[field, PEERS, pl.ds(block * 4, 4), :] = lines[field][numbers[0, me * 8 + block]]
        lost[field, HALO + me] = packed[field, PEERS]
        for i in range(PEERS + 1):
            for way in range(2):
                wrapped(field, i, way, "start")

    def wrapped(field, i, way, action):
        wrap, neighbour, first, to = wraps[way]
        peer = me if i == PEERS else peers[i]
        layer = me - first

        @pl.when(jnp.logical_and(wrap, jnp.logical_and(layer >= 0, layer < HALO)))
        def _():
            copy = pltpu.make_async_remote_copy(
                src_ref=packed.at[field, i],
                dst_ref=lost.at[field, me + to],
                send_sem=wrap_send.at[field, i],
                recv_sem=wrap_recv.at[field, way, layer],
                device_id={"slab": neighbour, "buddy": peer},
                device_id_type=MESH,
            )
            copy.start() if action == "start" else copy.wait_send()

    def to_buffer(buffer):
        def write(z, results):
            for field in range(FIELDS):
                buffer[field, z] = results[field]

        return write

    def to_advanced(z, results):
        results = [results[0] + results[4]] + results[1:]
        for field in range(FIELDS):
            advanced[z - HALO, field] = results[field]

    share = coefficients_ref[0, 0]
    live_share = coefficients_ref[0, 1]

    def to_recovered(z, results):
        results = [results[0] + results[4]] + results[1:]
        for field in range(FIELDS):
            recovered[field, z - HALO] = results[field]
            weighted[(z - HALO) // 2, (z - HALO) % 2, field] = share * results[field] + live_share * advanced[z - HALO, field]

    def to_weighted(z, results):
        results = [results[0] + results[4]] + results[1:]
        for field in range(FIELDS):
            weighted[(z - HALO) // 2, (z - HALO) % 2, field] = (
                share * recovered[field, z - HALO] + live_share * results[field]
            )

    def run_sections(state, scalars, finish):
        section(state, state, scalars, 0.25, 1, 2 * HALO + CZ - 2, to_buffer(stage_a), entry=True)
        section(stage_a, state, scalars, 1.0 / 3.0, 2, 2 * HALO + CZ - 4, to_buffer(stage_b))
        section(stage_b, state, scalars, 0.5, 3, 2 * HALO + CZ - 6, to_buffer(stage_a))
        section(stage_a, state, scalars, 1.0, HALO, CZ, finish)

    def pass_halos(field):
        for i in range(PEERS):
            second_copies[field * PEERS + i].wait_recv()
        for way in range(2):
            halo(field, way, "start")

    def halo(field, way, action):
        wrap, neighbour, first, to = wraps[way]

        def copy():
            return pltpu.make_async_remote_copy(
                src_ref=lost.at[field, pl.ds(HALO + first, HALO)],
                dst_ref=lost.at[field, pl.ds(first + to, HALO)],
                send_sem=halo_send.at[field, way],
                recv_sem=halo_recv.at[field, way],
                device_id={"slab": neighbour},
                device_id_type=MESH,
            )

        if action == "start" or action == "sent":

            @pl.when(jnp.logical_not(wrap))
            def _():
                copy().start() if action == "start" else copy().wait_send()

        else:
            far = wraps[1 - way][0]

            @pl.when(jnp.logical_not(far))
            def _():
                copy().wait_recv()

            @pl.when(far)
            def _():
                for layer in range(HALO):
                    pltpu.make_async_remote_copy(
                        src_ref=packed.at[field, 0],
                        dst_ref=lost.at[field, first + to + layer],
                        send_sem=wrap_send.at[field, 0],
                        recv_sem=wrap_recv.at[field, way, layer],
                        device_id={"slab": neighbour},
                        device_id_type=MESH,
                    ).wait_recv()

    live_scalars = stencil(levels_ref, 1)
    lost_scalars = stencil(levels_ref, 0)

    def live_section(step, first, count, finish):
        source, share_of_step, write = (
            (live, 0.25, to_buffer(live_a)),
            (live_a, 1.0 / 3.0, to_buffer(live_b)),
            (live_b, 0.5, to_buffer(live_a)),
            (live_a, 1.0, finish),
        )[step]
        section(source, live, live_scalars, share_of_step, first, count, write, entry=step == 0)

    late_below = slab % 8 == 0

    def live_received(late):
        for way in range(2):
            far = wraps[1 - way][0]

            @pl.when(far if late else jnp.logical_not(far))
            def _():
                live_copy(way).wait_recv()

    def early_live(step):
        if step == 0:
            live_received(False)

        @pl.when(jnp.logical_not(crossing))
        def _():
            live_section(step, 1 + step, 2 * HALO + CZ - 2 - 2 * step, to_advanced)

        @pl.when(crossing)
        def _():
            first = jnp.where(late_below, HALO + 1 + step, 1 + step)
            live_section(step, first, HALO + CZ - 2 - 2 * step, to_advanced)

    def late_live():
        live_received(True)

        @pl.when(crossing)
        def _():
            for step in range(4):
                first = jnp.where(late_below, 1 + step, HALO + CZ - 1 - step)
                live_section(step, first, HALO, to_weighted)

    pass_layers(0)
    pass_layers(1)
    pass_layers(2)
    pass_halos(0)
    pass_layers(3)
    pass_halos(1)
    pass_layers(4)
    live_in.wait()
    early_live(0)
    pass_halos(2)
    early_live(1)
    early_live(2)
    pass_halos(3)
    early_live(3)
    start_live(True)
    pass_halos(4)
    for field in range(FIELDS):
        for way in range(2):
            halo(field, way, "received")
    run_sections(lost, lost_scalars, to_recovered)

    third_copies = {}
    for field in range(FIELDS):
        for i, peer in enumerate(peers):
            third_copies[field, i] = pltpu.make_async_remote_copy(
                src_ref=weighted.at[peer // 2, peer % 2, field],
                dst_ref=arrived.at[field, i],
                send_sem=send3.at[field, i],
                recv_sem=recv3.at[field, i],
                device_id={"buddy": peer},
                device_id_type=MESH,
            )

    def send_layers(late):
        for field in range(FIELDS):
            for i, peer in enumerate(peers):
                is_late = jnp.logical_and(crossing, (peer < HALO) == late_below)

                @pl.when(is_late if late else jnp.logical_not(is_late))
                def _():
                    third_copies[field, i].start()

    send_layers(False)
    late_live()
    send_layers(True)

    recovered_out = pltpu.make_async_copy(recovered, recovered_ref, local_sem.at[0])
    recovered_out.start()

    for field in range(FIELDS):
        total[field, 16] = jnp.zeros((2, CX), jnp.float32)
    fourth_copies = []
    for field in range(FIELDS):
        summed = weighted[row, half, field]
        for i in range(PEERS):
            third_copies[field, i].wait_recv()
            summed = summed + arrived[field, i]
        for tile in range(16):
            total[field, tile] = summed[2 * tile : 2 * tile + 2]
        for i, peer in enumerate(peers):
            for rank in range(4):
                chosen[field, i, rank] = total[field, numbers[8, peer * 4 + rank]]
            copy = pltpu.make_async_remote_copy(
                src_ref=chosen.at[field, i],
                dst_ref=combined_ref.at[:, field, me],
                send_sem=send4.at[field, i],
                recv_sem=recv4.at[field, i],
                device_id={"buddy": peer},
                device_id_type=MESH,
            )
            copy.start()
            fourth_copies.append(copy)
        for rank in range(4):
            combined_ref[rank, field, me] = total[field, numbers[8, me * 4 + rank]]

    recovered_out.wait()
    for copy in fourth_copies:
        copy.wait()
    for copy in first_copies + second_copies + list(third_copies.values()):
        copy.wait_send()
    for way in range(2):
        live_copy(way).wait_send()
    for field in range(FIELDS):
        for way in range(2):
            halo(field, way, "sent")
            for i in range(PEERS + 1):
                wrapped(field, i, way, "sent")


def hand_over(recovered, combined):
    def copies(recovered_in, combined_in, recovered_out, combined_out, fields, tiles, sem_in, sem_out):
        pairs = [
            (recovered_in.at[0, field], fields.at[field], recovered_out.at[0, field]) for field in range(FIELDS)
        ] + [(combined_in, tiles, combined_out)]
        first = [
            pltpu.make_async_copy(pair[0], pair[1], sem_in.at[i]) for i, pair in enumerate(pairs)
        ]
        second = [
            pltpu.make_async_copy(pair[1], pair[2], sem_out.at[i]) for i, pair in enumerate(pairs)
        ]
        for copy in first:
            copy.start()
        for before, after in zip(first, second):
            before.wait()
            after.start()
        for copy in second:
            copy.wait()

    away = pl.BlockSpec(memory_space=pltpu.HBM)
    return pl.pallas_call(
        copies,
        name="hand_over",
        out_shape=(
            jax.ShapeDtypeStruct(recovered.shape, recovered.dtype),
            jax.ShapeDtypeStruct(combined.shape, combined.dtype),
        ),
        in_specs=[away, away],
        out_specs=(away, away),
        scratch_shapes=[
            pltpu.VMEM(recovered.shape[1:], jnp.float32),
            pltpu.VMEM(combined.shape, jnp.float32),
            pltpu.SemaphoreType.DMA((FIELDS + 1,)),
            pltpu.SemaphoreType.DMA((FIELDS + 1,)),
        ],
        compiler_params=pltpu.CompilerParams(vmem_limit_bytes=63 << 20),
    )(recovered, combined)


def body(checkpoint, slot_block, live_state, levels, coefficients, tile_owner):
    smem = pl.BlockSpec(memory_space=pltpu.SMEM)
    away = pl.BlockSpec(memory_space=pltpu.HBM)
    dma = pltpu.SemaphoreType.DMA
    recovered, combined = pl.pallas_call(
        kernel,
        name="recover_and_combine",
        out_shape=(
            jax.ShapeDtypeStruct((FIELDS, CZ, CY, CX), jnp.float32),
            jax.ShapeDtypeStruct((4, FIELDS, CZ, 2, CX), jnp.float32),
        ),
        in_specs=[smem, smem, smem, smem, away, away],
        out_specs=(away, pl.BlockSpec(memory_space=pltpu.VMEM)),
        scratch_shapes=[
            *[pltpu.VMEM((64, 4, CX), jnp.float32) for _ in range(FIELDS)],
            pltpu.VMEM((FIELDS, PEERS + 1, CY, CX), jnp.float32),
            pltpu.VMEM((FIELDS, CZ + 2 * HALO, CY, CX), jnp.float32),
            pltpu.VMEM((FIELDS, CZ + 2 * HALO, CY, CX), jnp.float32),
            pltpu.VMEM((FIELDS, CZ + 2 * HALO, CY, CX), jnp.float32),
            pltpu.VMEM((FIELDS, CZ + 2 * HALO, CY, CX), jnp.float32),
            pltpu.VMEM((FIELDS, CZ + 2 * HALO, CY, CX), jnp.float32),
            pltpu.VMEM((FIELDS, CZ + 2 * HALO, CY, CX), jnp.float32),
            pltpu.VMEM((CZ, FIELDS, CY, CX), jnp.float32),
            pltpu.VMEM((FIELDS, CZ, CY, CX), jnp.float32),
            pltpu.VMEM((4, 2, FIELDS, CY, CX), jnp.float32),
            pltpu.VMEM((FIELDS, PEERS, CY, CX), jnp.float32),
            pltpu.VMEM((FIELDS, 17, 2, CX), jnp.float32),
            pltpu.VMEM((FIELDS, PEERS, 4, 2, CX), jnp.float32),
            pltpu.VMEM((16, 128), jnp.int32),
            pltpu.SMEM((16, 128), jnp.int32),
            dma((2 + FIELDS,)),
            dma((FIELDS, PEERS)),
            dma((FIELDS, PEERS)),
            dma((FIELDS, PEERS)),
            dma((FIELDS, PEERS)),
            dma((FIELDS, PEERS)),
            dma((FIELDS, PEERS)),
            dma((FIELDS, PEERS)),
            dma((FIELDS, PEERS)),
            dma((FIELDS, PEERS + 1)),
            dma((FIELDS, 2, HALO)),
            dma((FIELDS, 2)),
            dma((FIELDS, 2)),
            dma((2,)),
            dma((2,)),
        ],
        compiler_params=pltpu.CompilerParams(
            collective_id=0, has_side_effects=True, vmem_limit_bytes=63 << 20
        ),
    )(slot_block, tile_owner, levels, coefficients.reshape(1, 2), checkpoint, live_state)
    return hand_over(recovered[None], combined)


def solution(mesh):
    return jax.shard_map(
        body,
        mesh=mesh,
        in_specs=(
            P("buddy", None, "slab", None, None),
            P(),
            P("buddy", None, "slab", None, None),
            P(None, "buddy", None),
            P(None, "buddy"),
            P("slab", None),
        ),
        out_specs=(P("buddy", None, "slab", None, None), P("buddy", None, "slab", None, None)),
        check_vma=False,
    )
```
